256 devices in a mesh: pair: 64 (over x, z, core), aux: 4 (over y).
Axes of the slice: x: 4, y: 4, z: 8, core: 2. Of those that a mesh axis runs over, the one named last changes fastest.
Arguments:
- factor: float32 [131072, 4096], P('pair', 'aux'), may hold values from -0.015625 to 0.015625
- trials: float32 [256, 131072], P('aux', 'pair'), may hold values from -6 to 6
- stored: float32 [384, 131072], P(None, 'pair'), may hold values from -0.015625 to 0.015625
- energy_gaps: float32 [131072], P('pair'), may hold values from 0.35 to 7
Outputs:
- next_trials: float32 [256, 131072], P('aux', 'pair')
- projections: float32 [2, 384, 256], P(None, None, 'aux')
The draws below stay inside these ranges and needn't reach their ends.
All inputs are finite; a program needn't handle non-finite values.
Results may differ from the reference program's by a relative error of at most 0.0001.
Values sent between devices are 32-bit elements; how exact they have to be, the bound alone decides.
A program may use at most 64 MiB of HBM per device.

```python
import jax
import jax.numpy as jnp
from jax import lax

PAIRS = 131072
AUX = 4096
STORED = 384
ROUNDS = 2
TRIALS = 256


def draw_energy_gaps(key, part):
    ramp = jnp.arange(PAIRS, dtype=jnp.float32) / PAIRS
    jitter = jax.random.uniform(jax.random.fold_in(key, 7), (PAIRS,), jnp.float32, 0.7, 1.4)
    return (0.5 + 4.5 * ramp) * jitter


def shard_levels(own_key, extent, pieces, smallest, largest):
    loudness = 1.0
    for position, parts in pieces:
        heights = jax.random.uniform(jax.random.fold_in(jax.random.fold_in(own_key, 6), position), (parts,), jnp.float32, smallest / len(pieces), largest / len(pieces))
        loudness = loudness * jnp.repeat(jnp.exp(heights), extent[position] // parts).reshape((-1,) + (1,) * (len(extent) - 1 - position))
    return loudness


def noise(key, dims, scale, bound, shards=(), held_as=jnp.bfloat16):
    array = jax.random.normal(key, dims, jnp.float32) * scale
    if len(shards) > 0:
        array = shard_levels(key, dims, shards, -0.22, 0.18) * array
    return jnp.clip(array, min=-bound, max=bound).astype(held_as)


def setup_inputs(seed: int = 0) -> dict:
    keys = jax.random.split(jax.random.key(seed), 5)
    factor = noise(keys[0], (PAIRS, AUX), PAIRS ** -0.5, 0.015625, ((0, 64), (1, 4)), jnp.float32)
    trials = noise(keys[1], (TRIALS, PAIRS), 1.0, 6.0, ((0, 4), (1, 64)), jnp.float32)
    stored = noise(keys[2], (STORED, PAIRS), PAIRS ** -0.5, 0.015625, ((1, 64),), jnp.float32)
    energy_gaps = draw_energy_gaps(jax.random.fold_in(keys[4], 71), 0)
    return dict(factor=factor, trials=trials, stored=stored, energy_gaps=energy_gaps)


def reference(factor, trials, stored, energy_gaps):
    highest = lax.Precision.HIGHEST
    current = trials
    collected = []
    for turn_index in range(ROUNDS):
        fitted = jnp.dot(current, factor, precision=highest, preferred_element_type=jnp.float32)
        coulomb = lax.dot_general(fitted, factor, (((1,), (1,)), ((), ())), precision=highest, preferred_element_type=jnp.float32)
        response = energy_gaps[None, :] * current + 4.0 * coulomb
        projection = lax.dot_general(stored, response, (((1,), (1,)), ((), ())), precision=highest, preferred_element_type=jnp.float32)
        removed = lax.dot_general(projection, stored, (((0,), (0,)), ((), ())), precision=highest, preferred_element_type=jnp.float32)
        remainder = response - removed
        scaled = remainder / energy_gaps[None, :]
        row_norm = jnp.sqrt(lax.optimization_barrier(jnp.mean(scaled * scaled, axis=1, keepdims=True)) + 1e-06)
        current = scaled / row_norm
        collected.append(projection)
    return (current, jnp.stack(collected))
```

```python
import functools

import jax
import jax.numpy as jnp
from jax import lax
from jax.experimental import pallas as pl
from jax.experimental.pallas import tpu as pltpu
from jax.sharding import Mesh
from jax.sharding import PartitionSpec as P

PAIRS = 131072
ROUNDS = 2
CH = 2
MESH = pl.DeviceIdType.MESH
F32 = jnp.float32
BF16 = jnp.bfloat16
NT = (((1,), (1,)), ((), ()))
NN = (((1,), (0,)), ((), ()))


def halves(v):
    hi = v.astype(BF16)
    lo = (v - hi.astype(F32)).astype(BF16)
    return hi, lo


def dot(a, b, dims):
    return lax.dot_general(a, b, dims, preferred_element_type=F32)


def dot3(stacked, m, b_hi, b_lo, dims):
    both = dot(stacked, b_hi, dims)
    return both[:m] + both[m:] + dot(stacked[:m], b_lo, dims)


def kernel(nx, nz, total_pairs, factor, trials, stored, gaps, o_next, o_proj,
           f32v, fhi, flo, s32v, shi, slo, gapv,
           xg, xs, fp, fx, fsum, rbuf, piece, fit, fs, w, tbuf, win, resp, rs,
           pp, prx, psm, prz, pz, pfull, srx, sq1, srz, sq0,
           load_sem, ag_s, ag_r, cx_s, cx_r, pr_s, pr_r, pa_s, pa_r, cy_s, cy_r,
           ys_s, ys_r, px_s, px_r, pz_s, pz_r, py_s, py_r, qx_s, qx_r, qz_s, qz_r):
    rows, pairs = trials.shape
    aux = factor.shape[1]
    n_st = stored.shape[0]
    rc = rows // CH
    rh = rc // 2
    m = 4 * rc
    half = 2 * rc
    rb = half // nx
    cb = aux // nz
    nxz = nx * nz
    nxc = 2 * nx
    pr = rows // nxc
    x, z = lax.axis_index("x"), lax.axis_index("z")
    c, y = lax.axis_index("core"), lax.axis_index("aux")
    right, left = lax.rem(y + 1, 4), lax.rem(y + 3, 4)

    def at(x_=None, z_=None, c_=None, y_=None):
        pick = lambda v, d: d if v is None else v
        return (pick(x_, x), pick(z_, z), pick(c_, c), pick(y_, y))

    def plane(k):
        return at(x_=lax.rem(x + k // nz, nx), z_=lax.rem(z + k % nz, nz))

    def row_peer(k):
        return at(x_=lax.rem(x + k // 2, nx), c_=lax.rem(c + k % 2, 2))

    def z_peer(k):
        return at(z_=lax.rem(z + k, nz))

    def remote(src, dst, s, r, dev):
        return pltpu.make_async_remote_copy(
            src_ref=src, dst_ref=dst, send_sem=s, recv_sem=r, device_id=dev,
            device_id_type=MESH)

    def arrived(refs, sem):
        pltpu.make_async_copy(refs, refs, sem).wait()

    bar = pltpu.get_barrier_semaphore()

    def greet(dev):
        pl.semaphore_signal(bar, inc=1, device_id=dev, device_id_type=MESH)

    greet(at(y_=right))
    greet(at(y_=left))

    @pl.loop(1, nxz)
    def _(k):
        greet(plane(k))

    @pl.loop(0, nx)
    def _(k):
        greet(at(x_=lax.rem(x + k, nx), c_=1 - c))

    loads = []
    for ch in range(CH):
        loads.append(pltpu.make_async_copy(
            trials.at[pl.ds(ch * rc, rc)], xg.at[0, ch, 0], load_sem.at[ch]))
    gap_load = pltpu.make_async_copy(gaps, gapv, load_sem.at[2])
    nf = 4
    fr = pairs // nf
    f_loads = [pltpu.make_async_copy(
        factor.at[pl.ds(i * fr, fr)], f32v.at[pl.ds(i * fr, fr)], load_sem.at[4 + i])
        for i in range(nf)]
    s_load = pltpu.make_async_copy(stored, s32v, load_sem.at[3])
    for d in loads + [gap_load] + f_loads + [s_load]:
        d.start()
    for d in loads:
        d.wait()
    pl.semaphore_wait(bar, 2 + (nxz - 1) + nx)

    started = []

    def go(d):
        d.start()
        started.append(d)

    def ag_start(r, ch):
        own = xg.at[r, ch, 0]
        for i in range(2):
            lo, hi = pl.ds(i * rh, rh), pl.ds((1 - i) * rh, rh)
            go(remote(own.at[lo], xg.at[r, ch, 1, lo], ag_s.at[r, ch, i], ag_r.at[r, ch, i],
                      at(y_=right)))
            go(remote(own.at[hi], xg.at[r, ch, 2, hi], ag_s.at[r, ch, 3 - i],
                      ag_r.at[r, ch, 3 - i], at(y_=left)))

    def ag_landed(r, ch, slot, i, sem):
        part = xg.at[r, ch, slot, pl.ds(i * rh, rh)]
        remote(part, part, ag_s.at[r, ch, sem], ag_r.at[r, ch, sem], at(y_=right)).wait_recv()

    def ag_relay(r, ch):
        ag_landed(r, ch, 1, 0, 0)
        a = pl.ds(0, rh)
        go(remote(xg.at[r, ch, 1, a], xg.at[r, ch, 3, a], ag_s.at[r, ch, 4], ag_r.at[r, ch, 4],
                  at(y_=right)))
        ag_landed(r, ch, 2, 1, 3)
        b = pl.ds(rh, rh)
        go(remote(xg.at[r, ch, 2, b], xg.at[r, ch, 3, b], ag_s.at[r, ch, 5], ag_r.at[r, ch, 5],
                  at(y_=left)))

    def ag_finish(r, ch):
        ag_landed(r, ch, 1, 1, 1)
        ag_landed(r, ch, 2, 0, 2)
        ag_landed(r, ch, 3, 0, 4)
        ag_landed(r, ch, 3, 1, 5)

    def fitted_partial(r, ch):
        for s in range(4):
            hi, lo = halves(xg[r, ch, s])
            xs[pl.ds(s * rc, rc)] = hi
            xs[pl.ds(m + s * rc, rc)] = lo
        tn = min(256, aux)

        @pl.loop(0, aux // tn)
        def _(n):
            cols = pl.ds(pl.multiple_of(n * tn, tn), tn)
            fp[r, ch, :, cols] = dot3(xs[...], m, fhi[:, cols], flo[:, cols], NN)

    def ar_core(r, ch):
        mine = pl.ds(pl.multiple_of((1 - c) * half, half), half)
        go(remote(fp.at[r, ch, mine], fx.at[r, ch], cx_s.at[r, ch], cx_r.at[r, ch],
                  at(c_=1 - c)))

    def ar_scatter(r, ch):
        remote(fx.at[r, ch], fx.at[r, ch], cx_s.at[r, ch], cx_r.at[r, ch],
               at(c_=1 - c)).wait_recv()
        own = pl.ds(pl.multiple_of(c * half, half), half)
        fsum[r, ch] = fp[r, ch, own, :] + fx[r, ch]

        @pl.loop(1, nxz)
        def _(k):
            to = plane(k)
            src = fsum.at[r, ch, pl.ds(pl.multiple_of(to[0] * rb, rb), rb),
                          pl.ds(pl.multiple_of(to[1] * cb, cb), cb)]
            remote(src, rbuf.at[r, ch, k], pr_s.at[r, ch], pr_r.at[r, ch], to).start()

    def ar_gather(r, ch):
        arrived(rbuf.at[r, ch, pl.ds(1, nxz - 1)], pr_r.at[r, ch])
        total = fsum[r, ch, pl.ds(pl.multiple_of(x * rb, rb), rb),
                     pl.ds(pl.multiple_of(z * cb, cb), cb)]
        total = lax.fori_loop(1, nxz, lambda k, t: t + rbuf[r, ch, k], total)
        piece[r, ch] = total
        here = (pl.ds(pl.multiple_of(c * half + x * rb, rb), rb),
                pl.ds(pl.multiple_of(z * cb, cb), cb))
        fit[r, ch, here[0], here[1]] = total

        @pl.loop(1, nxz)
        def _(k):
            remote(piece.at[r, ch], fit.at[r, ch, here[0], here[1]], pa_s.at[r, ch],
                   pa_r.at[r, ch], plane(k)).start()

    def ar_swap(r, ch):
        arrived(rbuf.at[r, ch, pl.ds(1, nxz - 1)], pa_r.at[r, ch])
        own = fit.at[r, ch, pl.ds(pl.multiple_of(c * half, half), half)]
        go(remote(own, own, cy_s.at[r, ch], cy_r.at[r, ch], at(c_=1 - c)))

    def ar_finish(r, ch):
        other = fit.at[r, ch, pl.ds(pl.multiple_of((1 - c) * half, half), half)]
        remote(other, other, cy_s.at[r, ch], cy_r.at[r, ch], at(c_=1 - c)).wait_recv()

    def spread(r, ch):
        hi, lo = halves(fit[r, ch])
        fs[pl.ds(0, m)] = hi
        fs[pl.ds(m, m)] = lo
        tn = min(256, pairs)

        @pl.loop(0, pairs // tn)
        def _(n):
            cols = pl.ds(pl.multiple_of(n * tn, tn), tn)
            v = dot3(fs[...], m, fhi[cols, :], flo[cols, :], NT)
            for s in range(4):
                w[r, ch, s, :, cols] = v[s * rc:(s + 1) * rc]

    def rs_start(r, ch):
        a, b = pl.ds(0, rh), pl.ds(rh, rh)
        go(remote(w.at[r, ch, 3, a], tbuf.at[r, ch, 0], ys_s.at[r, ch, 0], ys_r.at[r, ch, 0],
                  at(y_=right)))
        go(remote(w.at[r, ch, 3, b], tbuf.at[r, ch, 1], ys_s.at[r, ch, 1], ys_r.at[r, ch, 1],
                  at(y_=left)))
        go(remote(w.at[r, ch, 2, b], win.at[r, ch, 0, b], ys_s.at[r, ch, 2], ys_r.at[r, ch, 2],
                  at(y_=right)))
        go(remote(w.at[r, ch, 1, a], win.at[r, ch, 1, a], ys_s.at[r, ch, 3], ys_r.at[r, ch, 3],
                  at(y_=left)))

    def rs_relay(r, ch):
        a, b = pl.ds(0, rh), pl.ds(rh, rh)
        remote(tbuf.at[r, ch, 0], tbuf.at[r, ch, 0], ys_s.at[r, ch, 0], ys_r.at[r, ch, 0],
               at(y_=right)).wait_recv()
        tbuf[r, ch, 0] = tbuf[r, ch, 0] + w[r, ch, 2, a]
        go(remote(tbuf.at[r, ch, 0], win.at[r, ch, 0, a], ys_s.at[r, ch, 4], ys_r.at[r, ch, 4],
                  at(y_=right)))
        remote(tbuf.at[r, ch, 1], tbuf.at[r, ch, 1], ys_s.at[r, ch, 1], ys_r.at[r, ch, 1],
               at(y_=left)).wait_recv()
        tbuf[r, ch, 1] = tbuf[r, ch, 1] + w[r, ch, 1, b]
        go(remote(tbuf.at[r, ch, 1], win.at[r, ch, 1, b], ys_s.at[r, ch, 5], ys_r.at[r, ch, 5],
                  at(y_=left)))

    def rs_finish(r, ch, inv):
        a, b = pl.ds(0, rh), pl.ds(rh, rh)
        for side, part, sem in ((0, b, 2), (1, a, 3), (0, a, 4), (1, b, 5)):
            ref = win.at[r, ch, side, part]
            remote(ref, ref, ys_s.at[r, ch, sem], ys_r.at[r, ch, sem], at(y_=right)).wait_recv()
        value = gapv[...] * xg[r, ch, 0] + 4.0 * (w[r, ch, 0] + win[r, ch, 0] + win[r, ch, 1])
        if inv is not None:
            value = value * inv[ch * rc:(ch + 1) * rc]
        resp[pl.ds(ch * rc, rc)] = value
        hi, lo = halves(value)
        rs[pl.ds(0, rc)] = hi
        rs[pl.ds(rc, rc)] = lo
        pp[r, pl.ds(ch * rc, rc)] = dot3(rs[...], rc, shi[...], slo[...], NT)

    def proj_start(r):
        @pl.loop(1, nxc)
        def _(k):
            to = row_peer(k)
            src = pp.at[r, pl.ds(pl.multiple_of((to[0] * 2 + to[2]) * pr, pr), pr)]
            remote(src, prx.at[r, k], px_s.at[r], px_r.at[r], to).start()

        arrived(prx.at[r, pl.ds(1, nxc - 1)], px_r.at[r])
        mine = pl.ds(pl.multiple_of((x * 2 + c) * pr, pr), pr)
        total = lax.fori_loop(1, nxc, lambda k, t: t + prx[r, k], pp[r, mine, :])
        psm[r] = total
        prz[r, z] = total

        @pl.loop(1, nz)
        def _(k):
            remote(psm.at[r], prz.at[r, z], pz_s.at[r], pz_r.at[r], z_peer(k)).start()

    def proj_finish(r):
        arrived(prz.at[r, pl.ds(1, nz - 1)], pz_r.at[r])
        mine = pl.ds(pl.multiple_of((x * 2 + c) * pr, pr), pr)
        total = lax.fori_loop(1, nz, lambda k, t: t + prz[r, k], prz[r, 0])
        pz[r] = total
        pfull[r, mine, :] = total

        @pl.loop(1, nxc)
        def _(k):
            remote(pz.at[r], pfull.at[r, mine], py_s.at[r], py_r.at[r], row_peer(k)).start()

        arrived(prx.at[r, pl.ds(1, nxc - 1)], py_r.at[r])
        o_proj[r] = pfull[r]

    def removed(r, ch, dest):
        hi, lo = halves(pfull[r, pl.ds(ch * rc, rc)])
        p2 = jnp.concatenate([hi, lo], axis=0)
        tn = min(256, pairs)

        def step(n, acc):
            cols = pl.ds(pl.multiple_of(n * tn, tn), tn)
            v = dot3(p2, rc, shi[:, cols], slo[:, cols], NN)
            sc = (resp[pl.ds(ch * rc, rc), cols] - v) / gapv[:, cols]
            dest[:, cols] = sc
            return acc + jnp.sum(sc * sc, axis=1, keepdims=True)

        return lax.fori_loop(0, pairs // tn, step, jnp.zeros((rc, 1), F32))

    def squares_start(r, sums):
        lane = lax.broadcasted_iota(jnp.int32, (8, 128), 1)
        t = jnp.zeros((8, 128), F32)
        for g in range(rows // 8):
            t = jnp.where(lane == g, sums[8 * g:8 * g + 8], t)
        sq0[r] = t

        @pl.loop(1, nxc)
        def _(k):
            remote(sq0.at[r], srx.at[r, k], qx_s.at[r], qx_r.at[r], row_peer(k)).start()

    def squares_middle(r):
        arrived(srx.at[r, pl.ds(1, nxc - 1)], qx_r.at[r])
        sq1[r] = lax.fori_loop(1, nxc, lambda k, t: t + srx[r, k], sq0[r])

        @pl.loop(1, nz)
        def _(k):
            remote(sq1.at[r], srz.at[r, k], qz_s.at[r], qz_r.at[r], z_peer(k)).start()

    def inverse_norms(r):
        arrived(srz.at[r, pl.ds(1, nz - 1)], qz_r.at[r])
        t = lax.fori_loop(1, nz, lambda k, t: t + srz[r, k], sq1[r])
        inv = 1.0 / jnp.sqrt(t / total_pairs + 1e-06)
        return jnp.concatenate([inv[:, g:g + 1] for g in range(rows // 8)], axis=0)

    A, B = 0, 1
    inv = None
    for r in range(ROUNDS):
        if r == 0:
            ag_start(r, A)
            ag_relay(r, A)
            ag_start(r, B)
            gap_load.wait()
            for i, d in enumerate(f_loads):
                d.wait()
                tr = min(64, fr)

                @pl.loop(0, fr // tr)
                def _(t, i=i):
                    part = pl.ds(pl.multiple_of(i * fr + t * tr, tr), tr)
                    hi, lo = halves(f32v[part, :])
                    fhi[part, :] = hi
                    flo[part, :] = lo
        else:
            ag_relay(r, A)
        ag_finish(r, A)
        fitted_partial(r, A)
        ar_core(r, A)
        ag_relay(r, B)
        if r == 0:
            s_load.wait()
            ts = min(32, n_st)

            @pl.loop(0, n_st // ts)
            def _(t):
                part = pl.ds(pl.multiple_of(t * ts, ts), ts)
                hi, lo = halves(s32v[part, :])
                shi[part, :] = hi
                slo[part, :] = lo
        else:
            squares_middle(0)
        ar_scatter(r, A)
        ag_finish(r, B)
        fitted_partial(r, B)
        ar_core(r, B)
        ar_gather(r, A)
        ar_scatter(r, B)
        if r > 0:
            inv = inverse_norms(0)
        ar_swap(r, A)
        ar_gather(r, B)
        ar_finish(r, A)
        spread(r, A)
        rs_start(r, A)
        ar_swap(r, B)
        rs_relay(r, A)
        ar_finish(r, B)
        spread(r, B)
        rs_start(r, B)
        rs_finish(r, A, inv)
        rs_relay(r, B)
        rs_finish(r, B, inv)
        proj_start(r)
        proj_finish(r)
        if r + 1 < ROUNDS:
            sums = []
            for ch in range(CH):
                sums.append(removed(r, ch, xg.at[r + 1, ch, 0]))
                ag_start(r + 1, ch)
            squares_start(r, jnp.concatenate(sums, axis=0))
        else:
            sums = [removed(r, ch, o_next.at[pl.ds(ch * rc, rc)]) for ch in range(CH)]
            squares_start(r, jnp.concatenate(sums, axis=0))
            squares_middle(r)
            last = inverse_norms(r)
            o_next[...] = o_next[...] * last

    for d in started:
        d.wait_send()
    for r in range(ROUNDS):
        for ch in range(CH):
            arrived(rbuf.at[r, ch, pl.ds(1, nxz - 1)], pr_s.at[r, ch])
            arrived(rbuf.at[r, ch, pl.ds(1, nxz - 1)], pa_s.at[r, ch])
        arrived(prx.at[r, pl.ds(1, nxc - 1)], px_s.at[r])
        arrived(prz.at[r, pl.ds(1, nz - 1)], pz_s.at[r])
        arrived(prx.at[r, pl.ds(1, nxc - 1)], py_s.at[r])
        arrived(srx.at[r, pl.ds(1, nxc - 1)], qx_s.at[r])
        arrived(srz.at[r, pl.ds(1, nz - 1)], qz_s.at[r])


def on_device(nx, nz, total_pairs, factor, trials, stored, gaps):
    pairs, aux = factor.shape
    rows = trials.shape[0]
    n_st = stored.shape[0]
    rc = rows // CH
    m, half = 4 * rc, 2 * rc
    rb, cb = half // nx, aux // nz
    nxc = 2 * nx
    pr = rows // nxc
    V = pltpu.VMEM
    D = pltpu.SemaphoreType.DMA
    scratch = [
        V((pairs, aux), F32), V((pairs, aux), BF16), V((pairs, aux), BF16),
        V((n_st, pairs), F32), V((n_st, pairs), BF16), V((n_st, pairs), BF16),
        V((1, pairs), F32),
        V((ROUNDS, CH, 4, rc, pairs), F32),
        V((2 * m, pairs), BF16),
        V((ROUNDS, CH, m, aux), F32),
        V((ROUNDS, CH, half, aux), F32),
        V((ROUNDS, CH, half, aux), F32),
        V((ROUNDS, CH, nx * nz, rb, cb), F32),
        V((ROUNDS, CH, rb, cb), F32),
        V((ROUNDS, CH, m, aux), F32),
        V((2 * m, aux), BF16),
        V((ROUNDS, CH, 4, rc, pairs), F32),
        V((ROUNDS, CH, 2, rc // 2, pairs), F32),
        V((ROUNDS, CH, 2, rc, pairs), F32),
        V((rows, pairs), F32),
        V((2 * rc, pairs), BF16),
        V((ROUNDS, rows, n_st), F32),
        V((ROUNDS, nxc, pr, n_st), F32),
        V((ROUNDS, pr, n_st), F32),
        V((ROUNDS, nz, pr, n_st), F32),
        V((ROUNDS, pr, n_st), F32),
        V((ROUNDS, rows, n_st), F32),
        V((ROUNDS, nxc, 8, 128), F32),
        V((ROUNDS, 8, 128), F32),
        V((ROUNDS, nz, 8, 128), F32),
        V((ROUNDS, 8, 128), F32),
        D((8,)), D((ROUNDS, CH, 6)), D((ROUNDS, CH, 6)),
        D((ROUNDS, CH)), D((ROUNDS, CH)), D((ROUNDS, CH)), D((ROUNDS, CH)),
        D((ROUNDS, CH)), D((ROUNDS, CH)), D((ROUNDS, CH)), D((ROUNDS, CH)),
        D((ROUNDS, CH, 6)), D((ROUNDS, CH, 6)),
        D((ROUNDS,)), D((ROUNDS,)), D((ROUNDS,)), D((ROUNDS,)), D((ROUNDS,)), D((ROUNDS,)),
        D((ROUNDS,)), D((ROUNDS,)), D((ROUNDS,)), D((ROUNDS,)),
    ]
    any_spec = pl.BlockSpec(memory_space=pl.ANY)
    vmem_spec = pl.BlockSpec(memory_space=pltpu.VMEM)
    nxt, proj = pl.pallas_call(
        functools.partial(kernel, nx, nz, total_pairs),
        out_shape=(jax.ShapeDtypeStruct((rows, pairs), F32),
                   jax.ShapeDtypeStruct((ROUNDS, rows, n_st), F32)),
        in_specs=[any_spec] * 4,
        out_specs=(vmem_spec, vmem_spec),
        scratch_shapes=scratch,
        compiler_params=pltpu.CompilerParams(
            collective_id=0, has_side_effects=True, vmem_limit_bytes=66_000_000),
        name="response_rounds",
    )(factor, trials, stored, gaps.reshape(1, pairs))
    return nxt, jnp.swapaxes(proj, 1, 2)


def solution(mesh):
    nx, nz = 4, 8
    split = Mesh(
        mesh.devices.reshape(nx, nz, 2, mesh.shape["aux"]), ("x", "z", "core", "aux")
    )
    pair = ("x", "z", "core")
    return jax.shard_map(
        functools.partial(on_device, nx, nz, PAIRS),
        mesh=split,
        in_specs=(P(pair, "aux"), P("aux", pair), P(None, pair), P(pair)),
        out_specs=(P("aux", pair), P(None, None, "aux")),
        check_vma=False,
    )
```

```python
import functools

import jax
import jax.numpy as jnp
from jax import lax
from jax.experimental import pallas as pl
from jax.experimental.pallas import tpu as pltpu
from jax.sharding import Mesh
from jax.sharding import PartitionSpec as P

PAIRS = 131072
ROUNDS = 2
CH = 4
GR = 2
PER = CH // GR
MESH = pl.DeviceIdType.MESH
F32 = jnp.float32
BF16 = jnp.bfloat16
NT = (((1,), (1,)), ((), ()))
NN = (((1,), (0,)), ((), ()))
(
    FACTOR, TURN, STORED, SEND, RELAY, FIT, FIT_B, SCATTER, GATHER, SWAP, SPREAD, SPREAD_B,
    PASS, RESPOND, MEET, MEET_Z, MEET_ALL, REMOVE, SQUARES, SQUARES_Z, NORMS,
) = range(21)
ORDER = (
    (SEND, 0, 0), (RELAY, 0, 0), (FACTOR, 0, 1), (FACTOR, 0, 0), (SEND, 0, 1),
    (FACTOR, 0, 2), (TURN, 0, 2), (FACTOR, 0, 3), (FIT, 0, 0), (RELAY, 0, 1), (SEND, 0, 2),
    (FIT_B, 0, 0), (TURN, 0, 3), (SCATTER, 0, 0), (TURN, 0, 5), (FIT, 0, 1), (FIT_B, 0, 1),
    (SCATTER, 0, 1), (RELAY, 0, 2), (TURN, 0, 4), (SEND, 0, 3), (TURN, 0, 6), (TURN, 0, 1),
    (GATHER, 0, 0), (TURN, 0, 7), (TURN, 0, 0), (RELAY, 0, 3), (FIT, 0, 2), (GATHER, 0, 1),
    (FIT_B, 0, 2), (SCATTER, 0, 2), (FIT, 0, 3), (SWAP, 0, 0), (FIT_B, 0, 3),
    (SPREAD, 0, 0), (SPREAD_B, 0, 0), (SCATTER, 0, 3), (SWAP, 0, 1), (SPREAD, 0, 1),
    (SPREAD_B, 0, 1), (GATHER, 0, 2), (PASS, 0, 0), (PASS, 0, 1), (STORED, 0, 0),
    (GATHER, 0, 3), (RESPOND, 0, 0), (RESPOND, 0, 1), (MEET, 0, 0), (SWAP, 0, 2),
    (SPREAD, 0, 2), (SPREAD_B, 0, 2), (MEET_Z, 0, 0), (SWAP, 0, 3), (SPREAD, 0, 3),
    (SPREAD_B, 0, 3), (PASS, 0, 2), (MEET_ALL, 0, 0), (PASS, 0, 3), (REMOVE, 0, 0),
    (SEND, 1, 0), (RESPOND, 0, 2), (RESPOND, 0, 3), (MEET, 0, 1), (RELAY, 1, 0),
    (SEND, 1, 1), (MEET_Z, 0, 1), (FIT, 1, 0), (RELAY, 1, 1), (FIT_B, 1, 0),
    (MEET_ALL, 0, 1), (SCATTER, 1, 0), (FIT, 1, 1), (FIT_B, 1, 1), (REMOVE, 0, 1),
    (SEND, 1, 2), (SCATTER, 1, 1), (SQUARES, 0, 0), (RELAY, 1, 2), (SEND, 1, 3),
    (SQUARES_Z, 0, 0), (GATHER, 1, 0), (GATHER, 1, 1), (RELAY, 1, 3), (FIT, 1, 2),
    (FIT_B, 1, 2), (SCATTER, 1, 2), (NORMS, 0, 0), (SWAP, 1, 0), (FIT, 1, 3), (FIT_B, 1, 3),
    (SCATTER, 1, 3), (SPREAD, 1, 0), (SWAP, 1, 1), (SPREAD_B, 1, 0), (GATHER, 1, 2),
    (SPREAD, 1, 1), (SPREAD_B, 1, 1), (PASS, 1, 0), (GATHER, 1, 3), (PASS, 1, 1),
    (SWAP, 1, 2), (SPREAD, 1, 2), (SPREAD_B, 1, 2), (SWAP, 1, 3), (SPREAD, 1, 3),
    (SPREAD_B, 1, 3), (PASS, 1, 2), (RESPOND, 1, 0), (RESPOND, 1, 1), (MEET, 1, 0),
    (PASS, 1, 3), (RESPOND, 1, 2), (RESPOND, 1, 3), (MEET, 1, 1), (MEET_Z, 1, 0),
    (MEET_Z, 1, 1), (MEET_ALL, 1, 0), (MEET_ALL, 1, 1), (REMOVE, 1, 0), (REMOVE, 1, 1),
    (SQUARES, 1, 0), (SQUARES_Z, 1, 0), (NORMS, 1, 0),
)


def halves(v):
    hi = v.astype(BF16)
    lo = (v - hi.astype(F32)).astype(BF16)
    return hi, lo


def dot(a, b, dims):
    return lax.dot_general(a, b, dims, preferred_element_type=F32)


def dot3(stacked, m, b_hi, b_lo, dims):
    both = dot(stacked, b_hi, dims)
    return both[:m] + both[m:] + dot(stacked[:m], b_lo, dims)


def kernel(nx, nz, total_pairs, factor, trials, stored, gaps, o_next, o_proj,
           f32v, fhi, flo, fthi, ftlo, s32v, shi, slo, gapv,
           xg, xs, fp, fx, fsum, rbuf, piece, fit, fs, w, tbuf, win, resp, rs,
           pp, prx, psm, prz, pz, pfull, srx, sq1, srz, sq0, invn, sums,
           load_sem, ag_s, ag_r, cx_s, cx_r, pr_s, pr_r, pa_s, pa_r, cy_s, cy_r,
           ys_s, ys_r, px_s, px_r, pz_s, pz_r, py_s, py_r, qx_s, qx_r, qz_s, qz_r):
    rows, pairs = trials.shape
    aux = factor.shape[1]
    n_st = stored.shape[0]
    rc = rows // CH
    rh = rc // 2
    m = 4 * rc
    half = 2 * rc
    rb = half // nx
    cb = aux // nz
    nxz = nx * nz
    nxc = 2 * nx
    gr = rows // GR
    pr = gr // nx
    cw = pr_cols(n_st)
    x, z = lax.axis_index("x"), lax.axis_index("z")
    c, y = lax.axis_index("core"), lax.axis_index("aux")
    right, left = lax.rem(y + 1, 4), lax.rem(y + 3, 4)

    def at(x_=None, z_=None, c_=None, y_=None):
        pick = lambda v, d: d if v is None else v
        return (pick(x_, x), pick(z_, z), pick(c_, c), pick(y_, y))

    def plane(k):
        return at(x_=lax.rem(x + k // nz, nx), z_=lax.rem(z + k % nz, nz))

    def row_peer(k):
        return at(x_=lax.rem(x + k // 2, nx), c_=lax.rem(c + k % 2, 2))

    def z_peer(k):
        return at(z_=lax.rem(z + k, nz))

    def remote(src, dst, s, r, dev):
        return pltpu.make_async_remote_copy(
            src_ref=src, dst_ref=dst, send_sem=s, recv_sem=r, device_id=dev,
            device_id_type=MESH)

    def arrived(refs, sem):
        pltpu.make_async_copy(refs, refs, sem).wait()

    bar = pltpu.get_barrier_semaphore()

    def greet(dev):
        pl.semaphore_signal(bar, inc=1, device_id=dev, device_id_type=MESH)

    greet(at(y_=right))
    greet(at(y_=left))

    @pl.loop(1, nxz)
    def _(k):
        greet(plane(k))

    @pl.loop(0, nx)
    def _(k):
        greet(at(x_=lax.rem(x + k, nx), c_=1 - c))

    loads = []
    for ch in range(CH):
        loads.append(pltpu.make_async_copy(
            trials.at[pl.ds(ch * rc, rc)], xg.at[0, ch, 0], load_sem.at[ch]))
    gap_load = pltpu.make_async_copy(gaps, gapv, load_sem.at[CH])
    nf = 4
    fr = pairs // nf
    f_loads = [pltpu.make_async_copy(
        factor.at[pl.ds(i * fr, fr)], f32v.at[pl.ds(i * fr, fr)], load_sem.at[CH + 2 + i])
        for i in range(nf)]
    s_load = pltpu.make_async_copy(stored, s32v, load_sem.at[CH + 1])
    for d in loads + [gap_load] + f_loads + [s_load]:
        d.start()
    for d in loads:
        d.wait()
    pl.semaphore_wait(bar, 2 + (nxz - 1) + nx)

    started = []

    def go(d):
        d.start()
        started.append(d)

    def ag_start(r, ch):
        own = xg.at[r, ch, 0]
        for i in range(2):
            lo, hi = pl.ds(i * rh, rh), pl.ds((1 - i) * rh, rh)
            go(remote(own.at[lo], xg.at[r, ch, 1, lo], ag_s.at[r, ch, i], ag_r.at[r, ch, i],
                      at(y_=right)))
            go(remote(own.at[hi], xg.at[r, ch, 2, hi], ag_s.at[r, ch, 3 - i],
                      ag_r.at[r, ch, 3 - i], at(y_=left)))

    def ag_landed(r, ch, slot, i, sem):
        part = xg.at[r, ch, slot, pl.ds(i * rh, rh)]
        remote(part, part, ag_s.at[r, ch, sem], ag_r.at[r, ch, sem], at(y_=right)).wait_recv()

    def ag_relay(r, ch):
        ag_landed(r, ch, 1, 0, 0)
        a = pl.ds(0, rh)
        go(remote(xg.at[r, ch, 1, a], xg.at[r, ch, 3, a], ag_s.at[r, ch, 4], ag_r.at[r, ch, 4],
                  at(y_=right)))
        ag_landed(r, ch, 2, 1, 3)
        b = pl.ds(rh, rh)
        go(remote(xg.at[r, ch, 2, b], xg.at[r, ch, 3, b], ag_s.at[r, ch, 5], ag_r.at[r, ch, 5],
                  at(y_=left)))

    def ag_finish(r, ch):
        ag_landed(r, ch, 1, 1, 1)
        ag_landed(r, ch, 2, 0, 2)
        ag_landed(r, ch, 3, 0, 4)
        ag_landed(r, ch, 3, 1, 5)

    def fitted_partial(r, ch, part):
        if part == 0:
            for s in range(4):
                hi, lo = halves(xg[r, ch, s])
                xs[pl.ds(s * rc, rc)] = hi
                xs[pl.ds(m + s * rc, rc)] = lo
        tn = min(512, aux // 2)
        n_all = aux // tn

        @pl.loop(part * n_all // 2, (part + 1) * n_all // 2)
        def _(n):
            cols = pl.ds(pl.multiple_of(n * tn, tn), tn)
            fp[r, ch, :, cols] = dot3(xs[...], m, fhi[:, cols], flo[:, cols], NN)

    def ar_core(r, ch):
        mine = pl.ds(pl.multiple_of((1 - c) * half, half), half)
        go(remote(fp.at[r, ch, mine], fx.at[r, ch], cx_s.at[r, ch], cx_r.at[r, ch],
                  at(c_=1 - c)))

    def ar_scatter(r, ch):
        remote(fx.at[r, ch], fx.at[r, ch], cx_s.at[r, ch], cx_r.at[r, ch],
               at(c_=1 - c)).wait_recv()
        own = pl.ds(pl.multiple_of(c * half, half), half)
        fsum[r, ch] = fp[r, ch, own, :] + fx[r, ch]

        @pl.loop(1, nxz)
        def _(k):
            to = plane(k)
            src = fsum.at[r, ch, pl.ds(pl.multiple_of(to[0] * rb, rb), rb),
                          pl.ds(pl.multiple_of(to[1] * cb, cb), cb)]
            remote(src, rbuf.at[r, ch, k], pr_s.at[r, ch], pr_r.at[r, ch], to).start()

    def ar_gather(r, ch):
        arrived(rbuf.at[r, ch, pl.ds(1, nxz - 1)], pr_r.at[r, ch])
        total = fsum[r, ch, pl.ds(pl.multiple_of(x * rb, rb), rb),
                     pl.ds(pl.multiple_of(z * cb, cb), cb)]
        for k in range(1, nxz):
            total = total + rbuf[r, ch, k]
        piece[r, ch] = total
        here = (pl.ds(pl.multiple_of(c * half + x * rb, rb), rb),
                pl.ds(pl.multiple_of(z * cb, cb), cb))
        fit[r, ch, here[0], here[1]] = total

        @pl.loop(1, nxz)
        def _(k):
            remote(piece.at[r, ch], fit.at[r, ch, here[0], here[1]], pa_s.at[r, ch],
                   pa_r.at[r, ch], plane(k)).start()

    def ar_swap(r, ch):
        arrived(rbuf.at[r, ch, pl.ds(1, nxz - 1)], pa_r.at[r, ch])
        own = fit.at[r, ch, pl.ds(pl.multiple_of(c * half, half), half)]
        go(remote(own, own, cy_s.at[r, ch], cy_r.at[r, ch], at(c_=1 - c)))

    def ar_finish(r, ch):
        other = fit.at[r, ch, pl.ds(pl.multiple_of((1 - c) * half, half), half)]
        remote(other, other, cy_s.at[r, ch], cy_r.at[r, ch], at(c_=1 - c)).wait_recv()

    def spread(r, ch, part):
        if part == 0:
            hi, lo = halves(fit[r, ch])
            fs[pl.ds(0, m)] = hi
            fs[pl.ds(m, m)] = lo
        tn = min(512, pairs // 2)
        n_all = pairs // tn

        @pl.loop(part * n_all // 2, (part + 1) * n_all // 2)
        def _(n):
            cols = pl.ds(pl.multiple_of(n * tn, tn), tn)
            v = dot3(fs[...], m, fthi[:, cols], ftlo[:, cols], NN)
            for s in range(4):
                w[r, ch, s, :, cols] = v[s * rc:(s + 1) * rc]

    def rs_start(r, ch):
        a, b = pl.ds(0, rh), pl.ds(rh, rh)
        go(remote(w.at[r, ch, 3, a], tbuf.at[r, ch, 0], ys_s.at[r, ch, 0], ys_r.at[r, ch, 0],
                  at(y_=right)))
        go(remote(w.at[r, ch, 3, b], tbuf.at[r, ch, 1], ys_s.at[r, ch, 1], ys_r.at[r, ch, 1],
                  at(y_=left)))
        go(remote(w.at[r, ch, 2, b], win.at[r, ch, 0, b], ys_s.at[r, ch, 2], ys_r.at[r, ch, 2],
                  at(y_=right)))
        go(remote(w.at[r, ch, 1, a], win.at[r, ch, 1, a], ys_s.at[r, ch, 3], ys_r.at[r, ch, 3],
                  at(y_=left)))

    def rs_relay(r, ch):
        a, b = pl.ds(0, rh), pl.ds(rh, rh)
        remote(tbuf.at[r, ch, 0], tbuf.at[r, ch, 0], ys_s.at[r, ch, 0], ys_r.at[r, ch, 0],
               at(y_=right)).wait_recv()
        tbuf[r, ch, 0] = tbuf[r, ch, 0] + w[r, ch, 2, a]
        go(remote(tbuf.at[r, ch, 0], win.at[r, ch, 0, a], ys_s.at[r, ch, 4], ys_r.at[r, ch, 4],
                  at(y_=right)))
        remote(tbuf.at[r, ch, 1], tbuf.at[r, ch, 1], ys_s.at[r, ch, 1], ys_r.at[r, ch, 1],
               at(y_=left)).wait_recv()
        tbuf[r, ch, 1] = tbuf[r, ch, 1] + w[r, ch, 1, b]
        go(remote(tbuf.at[r, ch, 1], win.at[r, ch, 1, b], ys_s.at[r, ch, 5], ys_r.at[r, ch, 5],
                  at(y_=left)))

    def rs_finish(r, ch):
        a, b = pl.ds(0, rh), pl.ds(rh, rh)
        for side, part, sem in ((0, b, 2), (1, a, 3), (0, a, 4), (1, b, 5)):
            ref = win.at[r, ch, side, part]
            remote(ref, ref, ys_s.at[r, ch, sem], ys_r.at[r, ch, sem], at(y_=right)).wait_recv()
        mine = pl.ds(ch * rc, rc)
        value = gapv[...] * xg[r, ch, 0] + 4.0 * (w[r, ch, 0] + win[r, ch, 0] + win[r, ch, 1])
        if r > 0:
            value = value * invn[r - 1, mine, 0:1]
        resp[mine] = value
        hi, lo = halves(value)
        at_group = (ch % PER) * rc
        rs[pl.ds(at_group, rc)] = hi
        rs[pl.ds(gr + at_group, rc)] = lo

    def proj_start(r, g):
        pp[r, g, :, pl.ds(0, n_st)] = dot3(rs[...], gr, shi[...], slo[...], NT)
        if 2 * cw > n_st:
            pp[r, g, :, pl.ds(n_st, 2 * cw - n_st)] = jnp.zeros((gr, 2 * cw - n_st), F32)

        @pl.loop(1, nxc)
        def _(k):
            to = row_peer(k)
            src = pp.at[r, g, pl.ds(pl.multiple_of(to[0] * pr, pr), pr),
                        pl.ds(pl.multiple_of(to[2] * cw, cw), cw)]
            remote(src, prx.at[r, g, k], px_s.at[r, g], px_r.at[r, g], to).start()

    def proj_middle(r, g):
        arrived(prx.at[r, g, pl.ds(1, nxc - 1)], px_r.at[r, g])
        own = pp[r, g, pl.ds(pl.multiple_of(x * pr, pr), pr),
                 pl.ds(pl.multiple_of(c * cw, cw), cw)]
        for k in range(1, nxc):
            own = own + prx[r, g, k]
        psm[r, g] = own
        prz[r, g, z] = own

        @pl.loop(1, nz)
        def _(k):
            remote(psm.at[r, g], prz.at[r, g, z], pz_s.at[r, g], pz_r.at[r, g],
                   z_peer(k)).start()

    def proj_finish(r, g):
        arrived(prz.at[r, g, pl.ds(1, nz - 1)], pz_r.at[r, g])
        total = prz[r, g, 0]
        for k in range(1, nz):
            total = total + prz[r, g, k]
        pz[r, g] = total
        here = (pl.ds(pl.multiple_of(x * pr, pr), pr), pl.ds(pl.multiple_of(c * cw, cw), cw))
        pfull[r, g, here[0], here[1]] = total

        @pl.loop(1, nxc)
        def _(k):
            remote(pz.at[r, g], pfull.at[r, g, here[0], here[1]], py_s.at[r, g],
                   py_r.at[r, g], row_peer(k)).start()

    def proj_done(r, g):
        arrived(prx.at[r, g, pl.ds(1, nxc - 1)], py_r.at[r, g])
        o_proj[r, pl.ds(g * gr, gr)] = pfull[r, g, :, pl.ds(0, n_st)]

    def removed(r, g):
        mine = pl.ds(g * gr, gr)
        hi, lo = halves(pfull[r, g, :, pl.ds(0, n_st)])
        p2 = jnp.concatenate([hi, lo], axis=0)
        tn = min(512, pairs)

        def step(n, acc):
            cols = pl.ds(pl.multiple_of(n * tn, tn), tn)
            v = dot3(p2, gr, shi[:, cols], slo[:, cols], NN)
            sc = (resp[mine, cols] - v) / gapv[:, cols]
            if r + 1 < ROUNDS:
                for i in range(PER):
                    xg[r + 1, g * PER + i, 0, :, cols] = sc[i * rc:(i + 1) * rc]
            else:
                o_next[mine, cols] = sc
            return acc + jnp.sum(sc * sc, axis=1, keepdims=True)

        acc = lax.fori_loop(0, pairs // tn, step, jnp.zeros((gr, 1), F32))
        sums[r, mine] = jnp.broadcast_to(acc, (gr, 128))

    def squares_start(r):
        lane = lax.broadcasted_iota(jnp.int32, (8, 128), 1)
        t = jnp.zeros((8, 128), F32)
        for g in range(rows // 8):
            t = jnp.where(lane == g, sums[r, pl.ds(8 * g, 8)], t)
        sq0[r] = t

        @pl.loop(1, nxc)
        def _(k):
            remote(sq0.at[r], srx.at[r, k], qx_s.at[r], qx_r.at[r], row_peer(k)).start()

    def squares_middle(r):
        arrived(srx.at[r, pl.ds(1, nxc - 1)], qx_r.at[r])
        t = sq0[r]
        for k in range(1, nxc):
            t = t + srx[r, k]
        sq1[r] = t

        @pl.loop(1, nz)
        def _(k):
            remote(sq1.at[r], srz.at[r, k], qz_s.at[r], qz_r.at[r], z_peer(k)).start()

    def inverse_norms(r):
        arrived(srz.at[r, pl.ds(1, nz - 1)], qz_r.at[r])
        t = sq1[r]
        for k in range(1, nz):
            t = t + srz[r, k]
        inv = 1.0 / jnp.sqrt(t / total_pairs + 1e-06)
        for g in range(rows // 8):
            invn[r, pl.ds(8 * g, 8)] = jnp.broadcast_to(inv[:, g:g + 1], (8, 128))

    def split_factor(i):
        if i == 0:
            gap_load.wait()
        f_loads[i].wait()
        tr = min(64, fr)

        @pl.loop(0, fr // tr)
        def _(t):
            part = pl.ds(pl.multiple_of(i * fr + t * tr, tr), tr)
            hi, lo = halves(f32v[part, :])
            fhi[part, :] = hi
            flo[part, :] = lo

    def turn_factor(i):
        tp, ta = pairs // 8, min(256, aux)

        @pl.loop(0, aux // ta)
        def _(n):
            cols = pl.ds(pl.multiple_of(n * ta, ta), ta)
            hi, lo = halves(f32v[pl.ds(i * tp, tp), cols].T)
            fthi[cols, pl.ds(i * tp, tp)] = hi
            ftlo[cols, pl.ds(i * tp, tp)] = lo

    def split_stored():
        s_load.wait()
        ts = min(32, n_st)

        @pl.loop(0, n_st // ts)
        def _(t):
            part = pl.ds(pl.multiple_of(t * ts, ts), ts)
            hi, lo = halves(s32v[part, :])
            shi[part, :] = hi
            slo[part, :] = lo

    def last_spread(r, ch):
        spread(r, ch, 1)
        rs_start(r, ch)

    def last_fitted(r, ch):
        fitted_partial(r, ch, 1)
        ar_core(r, ch)

    def first_spread(r, ch):
        ar_finish(r, ch)
        spread(r, ch, 0)

    def first_fitted(r, ch):
        ag_finish(r, ch)
        fitted_partial(r, ch, 0)

    def remainder(r, g):
        proj_done(r, g)
        removed(r, g)

    stages = {
        FACTOR: lambda _, i: split_factor(i),
        TURN: lambda _, i: turn_factor(i),
        STORED: lambda *_: split_stored(),
        SEND: ag_start,
        RELAY: ag_relay,
        FIT: first_fitted,
        FIT_B: last_fitted,
        SCATTER: ar_scatter,
        GATHER: ar_gather,
        SWAP: ar_swap,
        SPREAD: first_spread,
        SPREAD_B: last_spread,
        PASS: rs_relay,
        RESPOND: rs_finish,
        MEET: proj_start,
        MEET_Z: proj_middle,
        MEET_ALL: proj_finish,
        REMOVE: remainder,
        SQUARES: lambda r, _: squares_start(r),
        SQUARES_Z: lambda r, _: squares_middle(r),
        NORMS: lambda r, _: inverse_norms(r),
    }
    for stage, r, i in ORDER:
        stages[stage](r, i)
    o_next[...] = o_next[...] * invn[ROUNDS - 1, :, 0:1]

    for d in started:
        d.wait_send()
    for r in range(ROUNDS):
        for ch in range(CH):
            arrived(rbuf.at[r, ch, pl.ds(1, nxz - 1)], pr_s.at[r, ch])
            arrived(rbuf.at[r, ch, pl.ds(1, nxz - 1)], pa_s.at[r, ch])
        for g in range(GR):
            arrived(prx.at[r, g, pl.ds(1, nxc - 1)], px_s.at[r, g])
            arrived(prz.at[r, g, pl.ds(1, nz - 1)], pz_s.at[r, g])
            arrived(prx.at[r, g, pl.ds(1, nxc - 1)], py_s.at[r, g])
        arrived(srx.at[r, pl.ds(1, nxc - 1)], qx_s.at[r])
        arrived(srz.at[r, pl.ds(1, nz - 1)], qz_s.at[r])


def pr_cols(n_st):
    return -(-n_st // 256) * 128


def on_device(nx, nz, total_pairs, factor, trials, stored, gaps):
    pairs, aux = factor.shape
    rows = trials.shape[0]
    n_st = stored.shape[0]
    rc = rows // CH
    m, half = 4 * rc, 2 * rc
    rb, cb = half // nx, aux // nz
    nxc = 2 * nx
    gr = rows // GR
    pr, cw = gr // nx, pr_cols(n_st)
    V = pltpu.VMEM
    D = pltpu.SemaphoreType.DMA
    scratch = [
        V((pairs, aux), F32), V((pairs, aux), BF16), V((pairs, aux), BF16),
        V((aux, pairs), BF16), V((aux, pairs), BF16),
        V((n_st, pairs), F32), V((n_st, pairs), BF16), V((n_st, pairs), BF16),
        V((1, pairs), F32),
        V((ROUNDS, CH, 4, rc, pairs), F32),
        V((2 * m, pairs), BF16),
        V((ROUNDS, CH, m, aux), F32),
        V((ROUNDS, CH, half, aux), F32),
        V((ROUNDS, CH, half, aux), F32),
        V((ROUNDS, CH, nx * nz, rb, cb), F32),
        V((ROUNDS, CH, rb, cb), F32),
        V((ROUNDS, CH, m, aux), F32),
        V((2 * m, aux), BF16),
        V((ROUNDS, CH, 4, rc, pairs), F32),
        V((ROUNDS, CH, 2, rc // 2, pairs), F32),
        V((ROUNDS, CH, 2, rc, pairs), F32),
        V((rows, pairs), F32),
        V((2 * gr, pairs), BF16),
        V((ROUNDS, GR, gr, 2 * cw), F32),
        V((ROUNDS, GR, nxc, pr, cw), F32),
        V((ROUNDS, GR, pr, cw), F32),
        V((ROUNDS, GR, nz, pr, cw), F32),
        V((ROUNDS, GR, pr, cw), F32),
        V((ROUNDS, GR, gr, 2 * cw), F32),
        V((ROUNDS, nxc, 8, 128), F32),
        V((ROUNDS, 8, 128), F32),
        V((ROUNDS, nz, 8, 128), F32),
        V((ROUNDS, 8, 128), F32),
        V((ROUNDS, rows, 128), F32),
        V((ROUNDS, rows, 128), F32),
        D((CH + 6,)), D((ROUNDS, CH, 6)), D((ROUNDS, CH, 6)),
        D((ROUNDS, CH)), D((ROUNDS, CH)), D((ROUNDS, CH)), D((ROUNDS, CH)),
        D((ROUNDS, CH)), D((ROUNDS, CH)), D((ROUNDS, CH)), D((ROUNDS, CH)),
        D((ROUNDS, CH, 6)), D((ROUNDS, CH, 6)),
        D((ROUNDS, GR)), D((ROUNDS, GR)), D((ROUNDS, GR)), D((ROUNDS, GR)),
        D((ROUNDS, GR)), D((ROUNDS, GR)),
        D((ROUNDS,)), D((ROUNDS,)), D((ROUNDS,)), D((ROUNDS,)),
    ]
    any_spec = pl.BlockSpec(memory_space=pl.ANY)
    vmem_spec = pl.BlockSpec(memory_space=pltpu.VMEM)
    nxt, proj = pl.pallas_call(
        functools.partial(kernel, nx, nz, total_pairs),
        out_shape=(jax.ShapeDtypeStruct((rows, pairs), F32),
                   jax.ShapeDtypeStruct((ROUNDS, rows, n_st), F32)),
        in_specs=[any_spec] * 4,
        out_specs=(vmem_spec, vmem_spec),
        scratch_shapes=scratch,
        compiler_params=pltpu.CompilerParams(
            collective_id=0, has_side_effects=True, vmem_limit_bytes=66_000_000),
        name="response_rounds",
    )(factor, trials, stored, gaps.reshape(1, pairs))
    return nxt, jnp.swapaxes(proj, 1, 2)


def solution(mesh):
    nx, nz = 4, 8
    split = Mesh(
        mesh.devices.reshape(nx, nz, 2, mesh.shape["aux"]), ("x", "z", "core", "aux")
    )
    pair = ("x", "z", "core")
    return jax.shard_map(
        functools.partial(on_device, nx, nz, PAIRS),
        mesh=split,
        in_specs=(P(pair, "aux"), P("aux", pair), P(None, pair), P(pair)),
        out_specs=(P("aux", pair), P(None, None, "aux")),
        check_vma=False,
    )
```

```python
import functools

import jax
import jax.numpy as jnp
from jax import lax
from jax.experimental import pallas as pl
from jax.experimental.pallas import tpu as pltpu
from jax.sharding import Mesh
from jax.sharding import PartitionSpec as P

PAIRS = 131072
ROUNDS = 2
CH = 4
GR = 2
PER = CH // GR
MESH = pl.DeviceIdType.MESH
F32 = jnp.float32
BF16 = jnp.bfloat16
NT = (((1,), (1,)), ((), ()))
NN = (((1,), (0,)), ((), ()))
(
    FACTOR, TURN, STORED, SEND, RELAY, FIT, FIT_B, SCATTER, GATHER, SWAP, SPREAD, SPREAD_B,
    PASS, RESPOND, MEET, MEET_Z, MEET_ALL, REMOVE, SQUARES, SQUARES_Z, NORMS,
) = range(21)
ORDER = (
    (SEND, 0, 0), (RELAY, 0, 0), (FACTOR, 0, 1), (FACTOR, 0, 0), (SEND, 0, 1),
    (FACTOR, 0, 2), (TURN, 0, 2), (FACTOR, 0, 3), (FIT, 0, 0), (RELAY, 0, 1), (SEND, 0, 2),
    (FIT_B, 0, 0), (TURN, 0, 3), (SCATTER, 0, 0), (TURN, 0, 5), (FIT, 0, 1), (FIT_B, 0, 1),
    (SCATTER, 0, 1), (RELAY, 0, 2), (TURN, 0, 4), (SEND, 0, 3), (TURN, 0, 6), (TURN, 0, 1),
    (GATHER, 0, 0), (TURN, 0, 7), (TURN, 0, 0), (RELAY, 0, 3), (FIT, 0, 2), (GATHER, 0, 1),
    (FIT_B, 0, 2), (SCATTER, 0, 2), (FIT, 0, 3), (SWAP, 0, 0), (FIT_B, 0, 3),
    (SPREAD, 0, 0), (SPREAD_B, 0, 0), (SCATTER, 0, 3), (SWAP, 0, 1), (SPREAD, 0, 1),
    (SPREAD_B, 0, 1), (GATHER, 0, 2), (PASS, 0, 0), (PASS, 0, 1), (STORED, 0, 0),
    (GATHER, 0, 3), (RESPOND, 0, 0), (RESPOND, 0, 1), (MEET, 0, 0), (SWAP, 0, 2),
    (SPREAD, 0, 2), (SPREAD_B, 0, 2), (MEET_Z, 0, 0), (SWAP, 0, 3), (SPREAD, 0, 3),
    (SPREAD_B, 0, 3), (PASS, 0, 2), (MEET_ALL, 0, 0), (PASS, 0, 3), (REMOVE, 0, 0),
    (SEND, 1, 0), (RESPOND, 0, 2), (RESPOND, 0, 3), (MEET, 0, 1), (RELAY, 1, 0),
    (SEND, 1, 1), (MEET_Z, 0, 1), (FIT, 1, 0), (RELAY, 1, 1), (FIT_B, 1, 0),
    (MEET_ALL, 0, 1), (SCATTER, 1, 0), (FIT, 1, 1), (FIT_B, 1, 1), (REMOVE, 0, 1),
    (SEND, 1, 2), (SCATTER, 1, 1), (SQUARES, 0, 0), (RELAY, 1, 2), (SEND, 1, 3),
    (SQUARES_Z, 0, 0), (GATHER, 1, 0), (GATHER, 1, 1), (RELAY, 1, 3), (FIT, 1, 2),
    (FIT_B, 1, 2), (SCATTER, 1, 2), (NORMS, 0, 0), (SWAP, 1, 0), (FIT, 1, 3), (FIT_B, 1, 3),
    (SCATTER, 1, 3), (SPREAD, 1, 0), (SWAP, 1, 1), (SPREAD_B, 1, 0), (GATHER, 1, 2),
    (SPREAD, 1, 1), (SPREAD_B, 1, 1), (PASS, 1, 0), (GATHER, 1, 3), (PASS, 1, 1),
    (SWAP, 1, 2), (SPREAD, 1, 2), (SPREAD_B, 1, 2), (SWAP, 1, 3), (SPREAD, 1, 3),
    (SPREAD_B, 1, 3), (PASS, 1, 2), (RESPOND, 1, 0), (RESPOND, 1, 1), (MEET, 1, 0),
    (PASS, 1, 3), (RESPOND, 1, 2), (RESPOND, 1, 3), (MEET, 1, 1), (MEET_Z, 1, 0),
    (MEET_Z, 1, 1), (MEET_ALL, 1, 0), (MEET_ALL, 1, 1), (REMOVE, 1, 0), (REMOVE, 1, 1),
    (SQUARES, 1, 0), (SQUARES_Z, 1, 0), (NORMS, 1, 0),
)


def halves(v):
    hi = v.astype(BF16)
    lo = (v - hi.astype(F32)).astype(BF16)
    return hi, lo


def dot(a, b, dims):
    return lax.dot_general(a, b, dims, preferred_element_type=F32)


def dot3(stacked, m, b_hi, b_lo, dims):
    both = dot(stacked, b_hi, dims)
    return both[:m] + both[m:] + dot(stacked[:m], b_lo, dims)


def kernel(nx, nz, total_pairs, factor, trials, stored, gaps, o_next, o_proj,
           f32v, fhi, flo, fthi, ftlo, s32v, shi, slo, gapv,
           xg, xs, fp, fx, fsum, rbuf, piece, fit, fs, w, tbuf, win, resp, rs,
           pp, prx, psm, prz, pz, pfull, srx, sq1, srz, sq0, invn, sums,
           load_sem, ag_s, ag_r, cx_s, cx_r, pr_s, pr_r, pa_s, pa_r, cy_s, cy_r,
           ys_s, ys_r, px_s, px_r, pz_s, pz_r, py_s, py_r, qx_s, qx_r, qz_s, qz_r):
    rows, pairs = trials.shape
    aux = factor.shape[1]
    n_st = stored.shape[0]
    rc = rows // CH
    rh = rc // 2
    m = 4 * rc
    half = 2 * rc
    rb = half // nx
    cb = aux // nz
    nxz = nx * nz
    nxc = 2 * nx
    gr = rows // GR
    pr = gr // nx
    cw = pr_cols(n_st)
    x, z = lax.axis_index("x"), lax.axis_index("z")
    c, y = lax.axis_index("core"), lax.axis_index("aux")
    right, left = lax.rem(y + 1, 4), lax.rem(y + 3, 4)

    def at(x_=None, z_=None, c_=None, y_=None):
        pick = lambda v, d: d if v is None else v
        return (pick(x_, x), pick(z_, z), pick(c_, c), pick(y_, y))

    def far_first(i, n):
        return n // 2 + (1 - 2 * (i % 2)) * ((i + 1) // 2)

    def plane_order(i):
        return far_first(i % nx, nx) * nz + far_first(i // nx, nz)

    def row_order(i):
        return far_first(i // 2, nx) * 2 + 1 - i % 2

    def plane(k):
        return at(x_=lax.rem(x + k // nz, nx), z_=lax.rem(z + k % nz, nz))

    def row_peer(k):
        return at(x_=lax.rem(x + k // 2, nx), c_=lax.rem(c + k % 2, 2))

    def z_peer(k):
        return at(z_=lax.rem(z + k, nz))

    def remote(src, dst, s, r, dev):
        return pltpu.make_async_remote_copy(
            src_ref=src, dst_ref=dst, send_sem=s, recv_sem=r, device_id=dev,
            device_id_type=MESH)

    def arrived(refs, sem):
        pltpu.make_async_copy(refs, refs, sem).wait()

    bar = pltpu.get_barrier_semaphore()

    def greet(dev):
        pl.semaphore_signal(bar, inc=1, device_id=dev, device_id_type=MESH)

    greet(at(y_=right))
    greet(at(y_=left))

    @pl.loop(1, nxz)
    def _(k):
        greet(plane(k))

    @pl.loop(0, nx)
    def _(k):
        greet(at(x_=lax.rem(x + k, nx), c_=1 - c))

    loads = []
    for ch in range(CH):
        loads.append(pltpu.make_async_copy(
            trials.at[pl.ds(ch * rc, rc)], xg.at[0, ch, 0], load_sem.at[ch]))
    gap_load = pltpu.make_async_copy(gaps, gapv, load_sem.at[CH])
    nf = 4
    fr = pairs // nf
    f_loads = [pltpu.make_async_copy(
        factor.at[pl.ds(i * fr, fr)], f32v.at[pl.ds(i * fr, fr)], load_sem.at[CH + 2 + i])
        for i in range(nf)]
    s_load = pltpu.make_async_copy(stored, s32v, load_sem.at[CH + 1])
    for d in loads + [gap_load] + f_loads + [s_load]:
        d.start()
    for d in loads:
        d.wait()
    pl.semaphore_wait(bar, 2 + (nxz - 1) + nx)

    started = []

    def go(d):
        d.start()
        started.append(d)

    def ag_start(r, ch):
        own = xg.at[r, ch, 0]
        for i in range(2):
            lo, hi = pl.ds(i * rh, rh), pl.ds((1 - i) * rh, rh)
            go(remote(own.at[lo], xg.at[r, ch, 1, lo], ag_s.at[r, ch, i], ag_r.at[r, ch, i],
                      at(y_=right)))
            go(remote(own.at[hi], xg.at[r, ch, 2, hi], ag_s.at[r, ch, 3 - i],
                      ag_r.at[r, ch, 3 - i], at(y_=left)))

    def ag_landed(r, ch, slot, i, sem):
        part = xg.at[r, ch, slot, pl.ds(i * rh, rh)]
        remote(part, part, ag_s.at[r, ch, sem], ag_r.at[r, ch, sem], at(y_=right)).wait_recv()

    def ag_relay(r, ch):
        ag_landed(r, ch, 1, 0, 0)
        a = pl.ds(0, rh)
        go(remote(xg.at[r, ch, 1, a], xg.at[r, ch, 3, a], ag_s.at[r, ch, 4], ag_r.at[r, ch, 4],
                  at(y_=right)))
        ag_landed(r, ch, 2, 1, 3)
        b = pl.ds(rh, rh)
        go(remote(xg.at[r, ch, 2, b], xg.at[r, ch, 3, b], ag_s.at[r, ch, 5], ag_r.at[r, ch, 5],
                  at(y_=left)))

    def ag_finish(r, ch):
        ag_landed(r, ch, 1, 1, 1)
        ag_landed(r, ch, 2, 0, 2)
        ag_landed(r, ch, 3, 0, 4)
        ag_landed(r, ch, 3, 1, 5)

    def fitted_partial(r, ch, part):
        if part == 0:
            for s in range(4):
                hi, lo = halves(xg[r, ch, s])
                xs[pl.ds(s * rc, rc)] = hi
                xs[pl.ds(m + s * rc, rc)] = lo
        tn = min(512, aux // 2)
        n_all = aux // tn

        @pl.loop(part * n_all // 2, (part + 1) * n_all // 2)
        def _(n):
            cols = pl.ds(pl.multiple_of(n * tn, tn), tn)
            fp[r, ch, :, cols] = dot3(xs[...], m, fhi[:, cols], flo[:, cols], NN)

    def ar_core(r, ch):
        mine = pl.ds(pl.multiple_of((1 - c) * half, half), half)
        go(remote(fp.at[r, ch, mine], fx.at[r, ch], cx_s.at[r, ch], cx_r.at[r, ch],
                  at(c_=1 - c)))

    def ar_scatter(r, ch):
        remote(fx.at[r, ch], fx.at[r, ch], cx_s.at[r, ch], cx_r.at[r, ch],
               at(c_=1 - c)).wait_recv()
        own = pl.ds(pl.multiple_of(c * half, half), half)
        fsum[r, ch] = fp[r, ch, own, :] + fx[r, ch]

        @pl.loop(0, nxz - 1)
        def _(i):
            k = plane_order(i)
            to = plane(k)
            src = fsum.at[r, ch, pl.ds(pl.multiple_of(to[0] * rb, rb), rb),
                          pl.ds(pl.multiple_of(to[1] * cb, cb), cb)]
            remote(src, rbuf.at[r, ch, k], pr_s.at[r, ch], pr_r.at[r, ch], to).start()

    def ar_gather(r, ch):
        arrived(rbuf.at[r, ch, pl.ds(1, nxz - 1)], pr_r.at[r, ch])
        total = fsum[r, ch, pl.ds(pl.multiple_of(x * rb, rb), rb),
                     pl.ds(pl.multiple_of(z * cb, cb), cb)]
        for k in range(1, nxz):
            total = total + rbuf[r, ch, k]
        piece[r, ch] = total
        here = (pl.ds(pl.multiple_of(c * half + x * rb, rb), rb),
                pl.ds(pl.multiple_of(z * cb, cb), cb))
        fit[r, ch, here[0], here[1]] = total

        @pl.loop(0, nxz - 1)
        def _(i):
            k = plane_order(i)
            remote(piece.at[r, ch], fit.at[r, ch, here[0], here[1]], pa_s.at[r, ch],
                   pa_r.at[r, ch], plane(k)).start()

    def ar_swap(r, ch):
        arrived(rbuf.at[r, ch, pl.ds(1, nxz - 1)], pa_r.at[r, ch])
        own = fit.at[r, ch, pl.ds(pl.multiple_of(c * half, half), half)]
        go(remote(own, own, cy_s.at[r, ch], cy_r.at[r, ch], at(c_=1 - c)))

    def ar_finish(r, ch):
        other = fit.at[r, ch, pl.ds(pl.multiple_of((1 - c) * half, half), half)]
        remote(other, other, cy_s.at[r, ch], cy_r.at[r, ch], at(c_=1 - c)).wait_recv()

    def spread(r, ch, part):
        if part == 0:
            hi, lo = halves(fit[r, ch])
            fs[pl.ds(0, m)] = hi
            fs[pl.ds(m, m)] = lo
        tn = min(512, pairs // 2)
        n_all = pairs // tn

        @pl.loop(part * n_all // 2, (part + 1) * n_all // 2)
        def _(n):
            cols = pl.ds(pl.multiple_of(n * tn, tn), tn)
            v = dot3(fs[...], m, fthi[:, cols], ftlo[:, cols], NN)
            for s in range(4):
                w[r, ch, s, :, cols] = v[s * rc:(s + 1) * rc]

    def rs_start(r, ch):
        a, b = pl.ds(0, rh), pl.ds(rh, rh)
        go(remote(w.at[r, ch, 3, a], tbuf.at[r, ch, 0], ys_s.at[r, ch, 0], ys_r.at[r, ch, 0],
                  at(y_=right)))
        go(remote(w.at[r, ch, 3, b], tbuf.at[r, ch, 1], ys_s.at[r, ch, 1], ys_r.at[r, ch, 1],
                  at(y_=left)))
        go(remote(w.at[r, ch, 2, b], win.at[r, ch, 0, b], ys_s.at[r, ch, 2], ys_r.at[r, ch, 2],
                  at(y_=right)))
        go(remote(w.at[r, ch, 1, a], win.at[r, ch, 1, a], ys_s.at[r, ch, 3], ys_r.at[r, ch, 3],
                  at(y_=left)))

    def rs_relay(r, ch):
        a, b = pl.ds(0, rh), pl.ds(rh, rh)
        remote(tbuf.at[r, ch, 0], tbuf.at[r, ch, 0], ys_s.at[r, ch, 0], ys_r.at[r, ch, 0],
               at(y_=right)).wait_recv()
        tbuf[r, ch, 0] = tbuf[r, ch, 0] + w[r, ch, 2, a]
        go(remote(tbuf.at[r, ch, 0], win.at[r, ch, 0, a], ys_s.at[r, ch, 4], ys_r.at[r, ch, 4],
                  at(y_=right)))
        remote(tbuf.at[r, ch, 1], tbuf.at[r, ch, 1], ys_s.at[r, ch, 1], ys_r.at[r, ch, 1],
               at(y_=left)).wait_recv()
        tbuf[r, ch, 1] = tbuf[r, ch, 1] + w[r, ch, 1, b]
        go(remote(tbuf.at[r, ch, 1], win.at[r, ch, 1, b], ys_s.at[r, ch, 5], ys_r.at[r, ch, 5],
                  at(y_=left)))

    def rs_finish(r, ch):
        a, b = pl.ds(0, rh), pl.ds(rh, rh)
        for side, part, sem in ((0, b, 2), (1, a, 3), (0, a, 4), (1, b, 5)):
            ref = win.at[r, ch, side, part]
            remote(ref, ref, ys_s.at[r, ch, sem], ys_r.at[r, ch, sem], at(y_=right)).wait_recv()
        mine = pl.ds(ch * rc, rc)
        value = gapv[...] * xg[r, ch, 0] + 4.0 * (w[r, ch, 0] + win[r, ch, 0] + win[r, ch, 1])
        if r > 0:
            value = value * invn[r - 1, mine, 0:1]
        resp[mine] = value
        hi, lo = halves(value)
        at_group = (ch % PER) * rc
        rs[pl.ds(at_group, rc)] = hi
        rs[pl.ds(gr + at_group, rc)] = lo

    def proj_start(r, g):
        pp[r, g, :, pl.ds(0, n_st)] = dot3(rs[...], gr, shi[...], slo[...], NT)
        if 2 * cw > n_st:
            pp[r, g, :, pl.ds(n_st, 2 * cw - n_st)] = jnp.zeros((gr, 2 * cw - n_st), F32)

        @pl.loop(0, nxc - 1)
        def _(i):
            k = row_order(i)
            to = row_peer(k)
            src = pp.at[r, g, pl.ds(pl.multiple_of(to[0] * pr, pr), pr),
                        pl.ds(pl.multiple_of(to[2] * cw, cw), cw)]
            remote(src, prx.at[r, g, k], px_s.at[r, g], px_r.at[r, g], to).start()

    def proj_middle(r, g):
        arrived(prx.at[r, g, pl.ds(1, nxc - 1)], px_r.at[r, g])
        own = pp[r, g, pl.ds(pl.multiple_of(x * pr, pr), pr),
                 pl.ds(pl.multiple_of(c * cw, cw), cw)]
        for k in range(1, nxc):
            own = own + prx[r, g, k]
        psm[r, g] = own
        prz[r, g, z] = own

        @pl.loop(0, nz - 1)
        def _(i):
            k = far_first(i, nz)
            remote(psm.at[r, g], prz.at[r, g, z], pz_s.at[r, g], pz_r.at[r, g],
                   z_peer(k)).start()

    def proj_finish(r, g):
        arrived(prz.at[r, g, pl.ds(1, nz - 1)], pz_r.at[r, g])
        total = prz[r, g, 0]
        for k in range(1, nz):
            total = total + prz[r, g, k]
        pz[r, g] = total
        here = (pl.ds(pl.multiple_of(x * pr, pr), pr), pl.ds(pl.multiple_of(c * cw, cw), cw))
        pfull[r, g, here[0], here[1]] = total

        @pl.loop(0, nxc - 1)
        def _(i):
            k = row_order(i)
            remote(pz.at[r, g], pfull.at[r, g, here[0], here[1]], py_s.at[r, g],
                   py_r.at[r, g], row_peer(k)).start()

    def proj_done(r, g):
        arrived(prx.at[r, g, pl.ds(1, nxc - 1)], py_r.at[r, g])
        o_proj[r, pl.ds(g * gr, gr)] = pfull[r, g, :, pl.ds(0, n_st)]

    def removed(r, g):
        mine = pl.ds(g * gr, gr)
        hi, lo = halves(pfull[r, g, :, pl.ds(0, n_st)])
        p2 = jnp.concatenate([hi, lo], axis=0)
        tn = min(512, pairs)

        def step(n, acc):
            cols = pl.ds(pl.multiple_of(n * tn, tn), tn)
            v = dot3(p2, gr, shi[:, cols], slo[:, cols], NN)
            sc = (resp[mine, cols] - v) / gapv[:, cols]
            if r + 1 < ROUNDS:
                for i in range(PER):
                    xg[r + 1, g * PER + i, 0, :, cols] = sc[i * rc:(i + 1) * rc]
            else:
                o_next[mine, cols] = sc
            return acc + jnp.sum(sc * sc, axis=1, keepdims=True)

        acc = lax.fori_loop(0, pairs // tn, step, jnp.zeros((gr, 1), F32))
        sums[r, mine] = jnp.broadcast_to(acc, (gr, 128))

    def squares_start(r):
        lane = lax.broadcasted_iota(jnp.int32, (8, 128), 1)
        t = jnp.zeros((8, 128), F32)
        for g in range(rows // 8):
            t = jnp.where(lane == g, sums[r, pl.ds(8 * g, 8)], t)
        sq0[r] = t

        @pl.loop(0, nxc - 1)
        def _(i):
            k = row_order(i)
            remote(sq0.at[r], srx.at[r, k], qx_s.at[r], qx_r.at[r], row_peer(k)).start()

    def squares_middle(r):
        arrived(srx.at[r, pl.ds(1, nxc - 1)], qx_r.at[r])
        t = sq0[r]
        for k in range(1, nxc):
            t = t + srx[r, k]
        sq1[r] = t

        @pl.loop(0, nz - 1)
        def _(i):
            k = far_first(i, nz)
            remote(sq1.at[r], srz.at[r, k], qz_s.at[r], qz_r.at[r], z_peer(k)).start()

    def inverse_norms(r):
        arrived(srz.at[r, pl.ds(1, nz - 1)], qz_r.at[r])
        t = sq1[r]
        for k in range(1, nz):
            t = t + srz[r, k]
        inv = 1.0 / jnp.sqrt(t / total_pairs + 1e-06)
        for g in range(rows // 8):
            invn[r, pl.ds(8 * g, 8)] = jnp.broadcast_to(inv[:, g:g + 1], (8, 128))

    def split_factor(i):
        if i == 0:
            gap_load.wait()
        f_loads[i].wait()
        tr = min(64, fr)

        @pl.loop(0, fr // tr)
        def _(t):
            part = pl.ds(pl.multiple_of(i * fr + t * tr, tr), tr)
            hi, lo = halves(f32v[part, :])
            fhi[part, :] = hi
            flo[part, :] = lo

    def turn_factor(i):
        tp, ta = pairs // 8, min(256, aux)

        @pl.loop(0, aux // ta)
        def _(n):
            cols = pl.ds(pl.multiple_of(n * ta, ta), ta)
            hi, lo = halves(f32v[pl.ds(i * tp, tp), cols].T)
            fthi[cols, pl.ds(i * tp, tp)] = hi
            ftlo[cols, pl.ds(i * tp, tp)] = lo

    def split_stored():
        s_load.wait()
        ts = min(32, n_st)

        @pl.loop(0, n_st // ts)
        def _(t):
            part = pl.ds(pl.multiple_of(t * ts, ts), ts)
            hi, lo = halves(s32v[part, :])
            shi[part, :] = hi
            slo[part, :] = lo

    def last_spread(r, ch):
        spread(r, ch, 1)
        rs_start(r, ch)

    def last_fitted(r, ch):
        fitted_partial(r, ch, 1)
        ar_core(r, ch)

    def first_spread(r, ch):
        ar_finish(r, ch)
        spread(r, ch, 0)

    def first_fitted(r, ch):
        ag_finish(r, ch)
        fitted_partial(r, ch, 0)

    def remainder(r, g):
        proj_done(r, g)
        removed(r, g)

    stages = {
        FACTOR: lambda _, i: split_factor(i),
        TURN: lambda _, i: turn_factor(i),
        STORED: lambda *_: split_stored(),
        SEND: ag_start,
        RELAY: ag_relay,
        FIT: first_fitted,
        FIT_B: last_fitted,
        SCATTER: ar_scatter,
        GATHER: ar_gather,
        SWAP: ar_swap,
        SPREAD: first_spread,
        SPREAD_B: last_spread,
        PASS: rs_relay,
        RESPOND: rs_finish,
        MEET: proj_start,
        MEET_Z: proj_middle,
        MEET_ALL: proj_finish,
        REMOVE: remainder,
        SQUARES: lambda r, _: squares_start(r),
        SQUARES_Z: lambda r, _: squares_middle(r),
        NORMS: lambda r, _: inverse_norms(r),
    }
    for stage, r, i in ORDER:
        stages[stage](r, i)
    o_next[...] = o_next[...] * invn[ROUNDS - 1, :, 0:1]

    for d in started:
        d.wait_send()
    for r in range(ROUNDS):
        for ch in range(CH):
            arrived(rbuf.at[r, ch, pl.ds(1, nxz - 1)], pr_s.at[r, ch])
            arrived(rbuf.at[r, ch, pl.ds(1, nxz - 1)], pa_s.at[r, ch])
        for g in range(GR):
            arrived(prx.at[r, g, pl.ds(1, nxc - 1)], px_s.at[r, g])
            arrived(prz.at[r, g, pl.ds(1, nz - 1)], pz_s.at[r, g])
            arrived(prx.at[r, g, pl.ds(1, nxc - 1)], py_s.at[r, g])
        arrived(srx.at[r, pl.ds(1, nxc - 1)], qx_s.at[r])
        arrived(srz.at[r, pl.ds(1, nz - 1)], qz_s.at[r])


def pr_cols(n_st):
    return -(-n_st // 256) * 128


def on_device(nx, nz, total_pairs, factor, trials, stored, gaps):
    pairs, aux = factor.shape
    rows = trials.shape[0]
    n_st = stored.shape[0]
    rc = rows // CH
    m, half = 4 * rc, 2 * rc
    rb, cb = half // nx, aux // nz
    nxc = 2 * nx
    gr = rows // GR
    pr, cw = gr // nx, pr_cols(n_st)
    V = pltpu.VMEM
    D = pltpu.SemaphoreType.DMA
    scratch = [
        V((pairs, aux), F32), V((pairs, aux), BF16), V((pairs, aux), BF16),
        V((aux, pairs), BF16), V((aux, pairs), BF16),
        V((n_st, pairs), F32), V((n_st, pairs), BF16), V((n_st, pairs), BF16),
        V((1, pairs), F32),
        V((ROUNDS, CH, 4, rc, pairs), F32),
        V((2 * m, pairs), BF16),
        V((ROUNDS, CH, m, aux), F32),
        V((ROUNDS, CH, half, aux), F32),
        V((ROUNDS, CH, half, aux), F32),
        V((ROUNDS, CH, nx * nz, rb, cb), F32),
        V((ROUNDS, CH, rb, cb), F32),
        V((ROUNDS, CH, m, aux), F32),
        V((2 * m, aux), BF16),
        V((ROUNDS, CH, 4, rc, pairs), F32),
        V((ROUNDS, CH, 2, rc // 2, pairs), F32),
        V((ROUNDS, CH, 2, rc, pairs), F32),
        V((rows, pairs), F32),
        V((2 * gr, pairs), BF16),
        V((ROUNDS, GR, gr, 2 * cw), F32),
        V((ROUNDS, GR, nxc, pr, cw), F32),
        V((ROUNDS, GR, pr, cw), F32),
        V((ROUNDS, GR, nz, pr, cw), F32),
        V((ROUNDS, GR, pr, cw), F32),
        V((ROUNDS, GR, gr, 2 * cw), F32),
        V((ROUNDS, nxc, 8, 128), F32),
        V((ROUNDS, 8, 128), F32),
        V((ROUNDS, nz, 8, 128), F32),
        V((ROUNDS, 8, 128), F32),
        V((ROUNDS, rows, 128), F32),
        V((ROUNDS, rows, 128), F32),
        D((CH + 6,)), D((ROUNDS, CH, 6)), D((ROUNDS, CH, 6)),
        D((ROUNDS, CH)), D((ROUNDS, CH)), D((ROUNDS, CH)), D((ROUNDS, CH)),
        D((ROUNDS, CH)), D((ROUNDS, CH)), D((ROUNDS, CH)), D((ROUNDS, CH)),
        D((ROUNDS, CH, 6)), D((ROUNDS, CH, 6)),
        D((ROUNDS, GR)), D((ROUNDS, GR)), D((ROUNDS, GR)), D((ROUNDS, GR)),
        D((ROUNDS, GR)), D((ROUNDS, GR)),
        D((ROUNDS,)), D((ROUNDS,)), D((ROUNDS,)), D((ROUNDS,)),
    ]
    any_spec = pl.BlockSpec(memory_space=pl.ANY)
    vmem_spec = pl.BlockSpec(memory_space=pltpu.VMEM)
    nxt, proj = pl.pallas_call(
        functools.partial(kernel, nx, nz, total_pairs),
        out_shape=(jax.ShapeDtypeStruct((rows, pairs), F32),
                   jax.ShapeDtypeStruct((ROUNDS, rows, n_st), F32)),
        in_specs=[any_spec] * 4,
        out_specs=(vmem_spec, vmem_spec),
        scratch_shapes=scratch,
        compiler_params=pltpu.CompilerParams(
            collective_id=0, has_side_effects=True, vmem_limit_bytes=66_000_000),
        name="response_rounds",
    )(factor, trials, stored, gaps.reshape(1, pairs))
    return nxt, jnp.swapaxes(proj, 1, 2)


def solution(mesh):
    nx, nz = 4, 8
    split = Mesh(
        mesh.devices.reshape(nx, nz, 2, mesh.shape["aux"]), ("x", "z", "core", "aux")
    )
    pair = ("x", "z", "core")
    return jax.shard_map(
        functools.partial(on_device, nx, nz, PAIRS),
        mesh=split,
        in_specs=(P(pair, "aux"), P("aux", pair), P(None, pair), P(pair)),
        out_specs=(P("aux", pair), P(None, None, "aux")),
        check_vma=False,
    )
```

```python
import functools

import jax
import jax.numpy as jnp
from jax import lax
from jax.experimental import pallas as pl
from jax.experimental.pallas import tpu as pltpu
from jax.sharding import Mesh
from jax.sharding import PartitionSpec as P

PAIRS = 131072
ROUNDS = 2
CH = 4
GR = 2
PER = CH // GR
MESH = pl.DeviceIdType.MESH
F32 = jnp.float32
BF16 = jnp.bfloat16
NT = (((1,), (1,)), ((), ()))
NN = (((1,), (0,)), ((), ()))
(
    FACTOR, TURN, STORED, SEND, RELAY, FIT, FIT_B, SCATTER, GATHER, SWAP, SPREAD, SPREAD_B,
    PASS, RESPOND, MEET, MEET_Z, MEET_ALL, REMOVE, SQUARES, SQUARES_Z, NORMS,
) = range(21)
ORDER = (
    (SEND, 0, 0), (RELAY, 0, 0), (FACTOR, 0, 1), (FACTOR, 0, 0), (SEND, 0, 1),
    (FACTOR, 0, 2), (TURN, 0, 2), (FACTOR, 0, 3), (FIT, 0, 0), (RELAY, 0, 1), (SEND, 0, 2),
    (FIT_B, 0, 0), (TURN, 0, 3), (SCATTER, 0, 0), (TURN, 0, 5), (FIT, 0, 1), (FIT_B, 0, 1),
    (SCATTER, 0, 1), (RELAY, 0, 2), (TURN, 0, 4), (SEND, 0, 3), (TURN, 0, 6), (TURN, 0, 1),
    (GATHER, 0, 0), (TURN, 0, 7), (TURN, 0, 0), (RELAY, 0, 3), (FIT, 0, 2), (GATHER, 0, 1),
    (FIT_B, 0, 2), (SCATTER, 0, 2), (FIT, 0, 3), (SWAP, 0, 0), (FIT_B, 0, 3),
    (SPREAD, 0, 0), (SPREAD_B, 0, 0), (SCATTER, 0, 3), (SWAP, 0, 1), (SPREAD, 0, 1),
    (SPREAD_B, 0, 1), (GATHER, 0, 2), (PASS, 0, 0), (PASS, 0, 1), (STORED, 0, 0),
    (GATHER, 0, 3), (RESPOND, 0, 0), (RESPOND, 0, 1), (MEET, 0, 0), (SWAP, 0, 2),
    (SPREAD, 0, 2), (SPREAD_B, 0, 2), (MEET_Z, 0, 0), (SWAP, 0, 3), (SPREAD, 0, 3),
    (SPREAD_B, 0, 3), (PASS, 0, 2), (MEET_ALL, 0, 0), (PASS, 0, 3), (REMOVE, 0, 0),
    (SEND, 1, 0), (RESPOND, 0, 2), (RESPOND, 0, 3), (MEET, 0, 1), (RELAY, 1, 0),
    (SEND, 1, 1), (MEET_Z, 0, 1), (FIT, 1, 0), (RELAY, 1, 1), (FIT_B, 1, 0),
    (MEET_ALL, 0, 1), (SCATTER, 1, 0), (FIT, 1, 1), (FIT_B, 1, 1), (REMOVE, 0, 1),
    (SEND, 1, 2), (SCATTER, 1, 1), (SQUARES, 0, 0), (RELAY, 1, 2), (SEND, 1, 3),
    (SQUARES_Z, 0, 0), (GATHER, 1, 0), (GATHER, 1, 1), (RELAY, 1, 3), (FIT, 1, 2),
    (FIT_B, 1, 2), (SCATTER, 1, 2), (NORMS, 0, 0), (SWAP, 1, 0), (FIT, 1, 3), (FIT_B, 1, 3),
    (SCATTER, 1, 3), (SPREAD, 1, 0), (SWAP, 1, 1), (SPREAD_B, 1, 0), (GATHER, 1, 2),
    (SPREAD, 1, 1), (SPREAD_B, 1, 1), (PASS, 1, 0), (GATHER, 1, 3), (PASS, 1, 1),
    (SWAP, 1, 2), (SPREAD, 1, 2), (SPREAD_B, 1, 2), (SWAP, 1, 3), (SPREAD, 1, 3),
    (SPREAD_B, 1, 3), (PASS, 1, 2), (RESPOND, 1, 0), (RESPOND, 1, 1), (MEET, 1, 0),
    (PASS, 1, 3), (RESPOND, 1, 2), (RESPOND, 1, 3), (MEET, 1, 1), (MEET_Z, 1, 0),
    (MEET_Z, 1, 1), (MEET_ALL, 1, 0), (MEET_ALL, 1, 1), (REMOVE, 1, 0), (REMOVE, 1, 1),
    (SQUARES, 1, 0), (SQUARES_Z, 1, 0), (NORMS, 1, 0),
)


def halves(v):
    hi = v.astype(BF16)
    lo = (v - hi.astype(F32)).astype(BF16)
    return hi, lo


def dot(a, b, dims):
    return lax.dot_general(a, b, dims, preferred_element_type=F32)


def dot3(stacked, m, b_hi, b_lo, dims):
    both = dot(stacked, b_hi, dims)
    return both[:m] + both[m:] + dot(stacked[:m], b_lo, dims)


def kernel(nx, nz, total_pairs, factor, trials, stored, gaps, o_next, o_proj,
           f32v, fhi, flo, fthi, ftlo, s32v, shi, slo, gapv,
           xg, xs, fp, fx, fsum, rbuf, piece, fit, fs, w, tbuf, win, resp, rs,
           pp, prx, psm, prz, pz, pfull, srx, sq1, srz, sq0, invn, sums,
           load_sem, ag_s, ag_r, cx_s, cx_r, pr_s, pr_r, pa_s, pa_r, cy_s, cy_r,
           ys_s, ys_r, px_s, px_r, pz_s, pz_r, py_s, py_r, qx_s, qx_r, qz_s, qz_r):
    rows, pairs = trials.shape
    aux = factor.shape[1]
    n_st = stored.shape[0]
    rc = rows // CH
    rh = rc // 2
    m = 4 * rc
    half = 2 * rc
    rb = half // nx
    cb = aux // nz
    nxz = nx * nz
    nxc = 2 * nx
    gr = rows // GR
    pr = gr // nx
    cw = pr_cols(n_st)
    x, z = lax.axis_index("x"), lax.axis_index("z")
    c, y = lax.axis_index("core"), lax.axis_index("aux")
    right, left = lax.rem(y + 1, 4), lax.rem(y + 3, 4)

    def at(x_=None, z_=None, c_=None, y_=None):
        pick = lambda v, d: d if v is None else v
        return (pick(x_, x), pick(z_, z), pick(c_, c), pick(y_, y))

    def plane(k):
        return at(x_=lax.rem(x + k // nz, nx), z_=lax.rem(z + k % nz, nz))

    def row_peer(k):
        return at(x_=lax.rem(x + k // 2, nx), c_=lax.rem(c + k % 2, 2))

    def z_peer(k):
        return at(z_=lax.rem(z + k, nz))

    def remote(src, dst, s, r, dev):
        return pltpu.make_async_remote_copy(
            src_ref=src, dst_ref=dst, send_sem=s, recv_sem=r, device_id=dev,
            device_id_type=MESH)

    def arrived(refs, sem):
        pltpu.make_async_copy(refs, refs, sem).wait()

    bar = pltpu.get_barrier_semaphore()

    def greet(dev):
        pl.semaphore_signal(bar, inc=1, device_id=dev, device_id_type=MESH)

    greet(at(y_=right))
    greet(at(y_=left))

    @pl.loop(1, nxz)
    def _(k):
        greet(plane(k))

    @pl.loop(0, nx)
    def _(k):
        greet(at(x_=lax.rem(x + k, nx), c_=1 - c))

    loads = []
    for ch in range(CH):
        loads.append(pltpu.make_async_copy(
            trials.at[pl.ds(ch * rc, rc)], xg.at[0, ch, 0], load_sem.at[ch]))
    gap_load = pltpu.make_async_copy(gaps, gapv, load_sem.at[CH])
    nf = 4
    fr = pairs // nf
    f_loads = [pltpu.make_async_copy(
        factor.at[pl.ds(i * fr, fr)], f32v.at[pl.ds(i * fr, fr)], load_sem.at[CH + 2 + i])
        for i in range(nf)]
    s_load = pltpu.make_async_copy(stored, s32v, load_sem.at[CH + 1])
    for d in loads + [gap_load] + f_loads + [s_load]:
        d.start()
    for d in loads:
        d.wait()
    pl.semaphore_wait(bar, 2 + (nxz - 1) + nx)

    started = []

    def go(d):
        d.start()
        started.append(d)

    def ag_start(r, ch):
        own = xg.at[r, ch, 0]
        for i in range(2):
            lo, hi = pl.ds(i * rh, rh), pl.ds((1 - i) * rh, rh)
            go(remote(own.at[lo], xg.at[r, ch, 1, lo], ag_s.at[r, ch, i], ag_r.at[r, ch, i],
                      at(y_=right)))
            go(remote(own.at[hi], xg.at[r, ch, 2, hi], ag_s.at[r, ch, 3 - i],
                      ag_r.at[r, ch, 3 - i], at(y_=left)))

    def ag_landed(r, ch, slot, i, sem):
        part = xg.at[r, ch, slot, pl.ds(i * rh, rh)]
        remote(part, part, ag_s.at[r, ch, sem], ag_r.at[r, ch, sem], at(y_=right)).wait_recv()

    def ag_relay(r, ch):
        ag_landed(r, ch, 1, 0, 0)
        a = pl.ds(0, rh)
        go(remote(xg.at[r, ch, 1, a], xg.at[r, ch, 3, a], ag_s.at[r, ch, 4], ag_r.at[r, ch, 4],
                  at(y_=right)))
        ag_landed(r, ch, 2, 1, 3)
        b = pl.ds(rh, rh)
        go(remote(xg.at[r, ch, 2, b], xg.at[r, ch, 3, b], ag_s.at[r, ch, 5], ag_r.at[r, ch, 5],
                  at(y_=left)))

    def ag_finish(r, ch):
        ag_landed(r, ch, 1, 1, 1)
        ag_landed(r, ch, 2, 0, 2)
        ag_landed(r, ch, 3, 0, 4)
        ag_landed(r, ch, 3, 1, 5)

    def fitted_partial(r, ch, part):
        if part == 0:
            for s in range(4):
                hi, lo = halves(xg[r, ch, s])
                xs[pl.ds(s * rc, rc)] = hi
                xs[pl.ds(m + s * rc, rc)] = lo
        tn = min(512, aux // 2)
        n_all = aux // tn

        @pl.loop(part * n_all // 2, (part + 1) * n_all // 2)
        def _(n):
            cols = pl.ds(pl.multiple_of(n * tn, tn), tn)
            fp[r, ch, :, cols] = dot3(xs[...], m, fhi[:, cols], flo[:, cols], NN)

    def ar_core(r, ch):
        mine = pl.ds(pl.multiple_of((1 - c) * half, half), half)
        go(remote(fp.at[r, ch, mine], fx.at[r, ch], cx_s.at[r, ch], cx_r.at[r, ch],
                  at(c_=1 - c)))

    def ar_scatter(r, ch):
        remote(fx.at[r, ch], fx.at[r, ch], cx_s.at[r, ch], cx_r.at[r, ch],
               at(c_=1 - c)).wait_recv()
        own = pl.ds(pl.multiple_of(c * half, half), half)
        fsum[r, ch] = fp[r, ch, own, :] + fx[r, ch]

        @pl.loop(1, nxz)
        def _(k):
            to = plane(k)
            src = fsum.at[r, ch, pl.ds(pl.multiple_of(to[0] * rb, rb), rb),
                          pl.ds(pl.multiple_of(to[1] * cb, cb), cb)]
            remote(src, rbuf.at[r, ch, k], pr_s.at[r, ch], pr_r.at[r, ch], to).start()

    def ar_gather(r, ch):
        arrived(rbuf.at[r, ch, pl.ds(1, nxz - 1)], pr_r.at[r, ch])
        total = fsum[r, ch, pl.ds(pl.multiple_of(x * rb, rb), rb),
                     pl.ds(pl.multiple_of(z * cb, cb), cb)]
        for k in range(1, nxz):
            total = total + rbuf[r, ch, k]
        piece[r, ch] = total
        here = (pl.ds(pl.multiple_of(c * half + x * rb, rb), rb),
                pl.ds(pl.multiple_of(z * cb, cb), cb))
        fit[r, ch, here[0], here[1]] = total

        @pl.loop(1, nxz)
        def _(k):
            remote(piece.at[r, ch], fit.at[r, ch, here[0], here[1]], pa_s.at[r, ch],
                   pa_r.at[r, ch], plane(k)).start()

    def ar_swap(r, ch):
        arrived(rbuf.at[r, ch, pl.ds(1, nxz - 1)], pa_r.at[r, ch])
        own = fit.at[r, ch, pl.ds(pl.multiple_of(c * half, half), half)]
        go(remote(own, own, cy_s.at[r, ch], cy_r.at[r, ch], at(c_=1 - c)))

    def ar_finish(r, ch):
        other = fit.at[r, ch, pl.ds(pl.multiple_of((1 - c) * half, half), half)]
        remote(other, other, cy_s.at[r, ch], cy_r.at[r, ch], at(c_=1 - c)).wait_recv()

    def spread(r, ch, part):
        if part == 0:
            hi, lo = halves(fit[r, ch])
            fs[pl.ds(0, m)] = hi
            fs[pl.ds(m, m)] = lo
        tn = min(512, pairs // 2)
        n_all = pairs // tn

        @pl.loop(part * n_all // 2, (part + 1) * n_all // 2)
        def _(n):
            cols = pl.ds(pl.multiple_of(n * tn, tn), tn)
            v = dot3(fs[...], m, fthi[:, cols], ftlo[:, cols], NN)
            for s in range(4):
                w[r, ch, s, :, cols] = v[s * rc:(s + 1) * rc]

    def rs_start(r, ch):
        a, b = pl.ds(0, rh), pl.ds(rh, rh)
        go(remote(w.at[r, ch, 3, a], tbuf.at[r, ch, 0], ys_s.at[r, ch, 0], ys_r.at[r, ch, 0],
                  at(y_=right)))
        go(remote(w.at[r, ch, 3, b], tbuf.at[r, ch, 1], ys_s.at[r, ch, 1], ys_r.at[r, ch, 1],
                  at(y_=left)))
        go(remote(w.at[r, ch, 2, b], win.at[r, ch, 0, b], ys_s.at[r, ch, 2], ys_r.at[r, ch, 2],
                  at(y_=right)))
        go(remote(w.at[r, ch, 1, a], win.at[r, ch, 1, a], ys_s.at[r, ch, 3], ys_r.at[r, ch, 3],
                  at(y_=left)))

    def rs_relay(r, ch):
        a, b = pl.ds(0, rh), pl.ds(rh, rh)
        remote(tbuf.at[r, ch, 0], tbuf.at[r, ch, 0], ys_s.at[r, ch, 0], ys_r.at[r, ch, 0],
               at(y_=right)).wait_recv()
        tbuf[r, ch, 0] = tbuf[r, ch, 0] + w[r, ch, 2, a]
        go(remote(tbuf.at[r, ch, 0], win.at[r, ch, 0, a], ys_s.at[r, ch, 4], ys_r.at[r, ch, 4],
                  at(y_=right)))
        remote(tbuf.at[r, ch, 1], tbuf.at[r, ch, 1], ys_s.at[r, ch, 1], ys_r.at[r, ch, 1],
               at(y_=left)).wait_recv()
        tbuf[r, ch, 1] = tbuf[r, ch, 1] + w[r, ch, 1, b]
        go(remote(tbuf.at[r, ch, 1], win.at[r, ch, 1, b], ys_s.at[r, ch, 5], ys_r.at[r, ch, 5],
                  at(y_=left)))

    def rs_finish(r, ch):
        a, b = pl.ds(0, rh), pl.ds(rh, rh)
        for side, part, sem in ((0, b, 2), (1, a, 3), (0, a, 4), (1, b, 5)):
            ref = win.at[r, ch, side, part]
            remote(ref, ref, ys_s.at[r, ch, sem], ys_r.at[r, ch, sem], at(y_=right)).wait_recv()
        mine = pl.ds(ch * rc, rc)
        value = gapv[...] * xg[r, ch, 0] + 4.0 * (w[r, ch, 0] + win[r, ch, 0] + win[r, ch, 1])
        if r > 0:
            value = value * invn[r - 1, mine, 0:1]
        resp[mine] = value
        hi, lo = halves(value)
        at_group = (ch % PER) * rc
        rs[pl.ds(at_group, rc)] = hi
        rs[pl.ds(gr + at_group, rc)] = lo

    def proj_start(r, g):
        pp[r, g, :, pl.ds(0, n_st)] = dot3(rs[...], gr, shi[...], slo[...], NT)
        if 2 * cw > n_st:
            pp[r, g, :, pl.ds(n_st, 2 * cw - n_st)] = jnp.zeros((gr, 2 * cw - n_st), F32)

        @pl.loop(1, nxc)
        def _(k):
            to = row_peer(k)
            src = pp.at[r, g, pl.ds(pl.multiple_of(to[0] * pr, pr), pr),
                        pl.ds(pl.multiple_of(to[2] * cw, cw), cw)]
            remote(src, prx.at[r, g, k], px_s.at[r, g], px_r.at[r, g], to).start()

    def proj_middle(r, g):
        arrived(prx.at[r, g, pl.ds(1, nxc - 1)], px_r.at[r, g])
        own = pp[r, g, pl.ds(pl.multiple_of(x * pr, pr), pr),
                 pl.ds(pl.multiple_of(c * cw, cw), cw)]
        for k in range(1, nxc):
            own = own + prx[r, g, k]
        psm[r, g] = own
        prz[r, g, z] = own

        @pl.loop(1, nz)
        def _(k):
            remote(psm.at[r, g], prz.at[r, g, z], pz_s.at[r, g], pz_r.at[r, g],
                   z_peer(k)).start()

    def proj_finish(r, g):
        arrived(prz.at[r, g, pl.ds(1, nz - 1)], pz_r.at[r, g])
        total = prz[r, g, 0]
        for k in range(1, nz):
            total = total + prz[r, g, k]
        pz[r, g] = total
        here = (pl.ds(pl.multiple_of(x * pr, pr), pr), pl.ds(pl.multiple_of(c * cw, cw), cw))
        pfull[r, g, here[0], here[1]] = total

        @pl.loop(1, nxc)
        def _(k):
            remote(pz.at[r, g], pfull.at[r, g, here[0], here[1]], py_s.at[r, g],
                   py_r.at[r, g], row_peer(k)).start()

    def proj_done(r, g):
        arrived(prx.at[r, g, pl.ds(1, nxc - 1)], py_r.at[r, g])
        o_proj[r, pl.ds(g * gr, gr)] = pfull[r, g, :, pl.ds(0, n_st)]

    def removed(r, g):
        mine = pl.ds(g * gr, gr)
        hi, lo = halves(pfull[r, g, :, pl.ds(0, n_st)])
        p2 = jnp.concatenate([hi, lo], axis=0)
        tn = min(1024, pairs)

        def step(n, acc):
            cols = pl.ds(pl.multiple_of(n * tn, tn), tn)
            v = dot3(p2, gr, shi[:, cols], slo[:, cols], NN)
            sc = (resp[mine, cols] - v) / gapv[:, cols]
            if r + 1 < ROUNDS:
                for i in range(PER):
                    xg[r + 1, g * PER + i, 0, :, cols] = sc[i * rc:(i + 1) * rc]
            else:
                o_next[mine, cols] = sc
            return acc + jnp.sum(sc * sc, axis=1, keepdims=True)

        acc = lax.fori_loop(0, pairs // tn, step, jnp.zeros((gr, 1), F32))
        sums[r, mine] = jnp.broadcast_to(acc, (gr, 128))

    def squares_start(r):
        lane = lax.broadcasted_iota(jnp.int32, (8, 128), 1)
        t = jnp.zeros((8, 128), F32)
        for g in range(rows // 8):
            t = jnp.where(lane == g, sums[r, pl.ds(8 * g, 8)], t)
        sq0[r] = t

        @pl.loop(1, nxc)
        def _(k):
            remote(sq0.at[r], srx.at[r, k], qx_s.at[r], qx_r.at[r], row_peer(k)).start()

    def squares_middle(r):
        arrived(srx.at[r, pl.ds(1, nxc - 1)], qx_r.at[r])
        t = sq0[r]
        for k in range(1, nxc):
            t = t + srx[r, k]
        sq1[r] = t

        @pl.loop(1, nz)
        def _(k):
            remote(sq1.at[r], srz.at[r, k], qz_s.at[r], qz_r.at[r], z_peer(k)).start()

    def inverse_norms(r):
        arrived(srz.at[r, pl.ds(1, nz - 1)], qz_r.at[r])
        t = sq1[r]
        for k in range(1, nz):
            t = t + srz[r, k]
        inv = 1.0 / jnp.sqrt(t / total_pairs + 1e-06)
        for g in range(rows // 8):
            invn[r, pl.ds(8 * g, 8)] = jnp.broadcast_to(inv[:, g:g + 1], (8, 128))

    def split_factor(i):
        if i == 0:
            gap_load.wait()
        f_loads[i].wait()
        tr = min(64, fr)

        @pl.loop(0, fr // tr)
        def _(t):
            part = pl.ds(pl.multiple_of(i * fr + t * tr, tr), tr)
            hi, lo = halves(f32v[part, :])
            fhi[part, :] = hi
            flo[part, :] = lo

    def turn_factor(i):
        tp, ta = pairs // 8, min(256, aux)

        @pl.loop(0, aux // ta)
        def _(n):
            cols = pl.ds(pl.multiple_of(n * ta, ta), ta)
            hi, lo = halves(f32v[pl.ds(i * tp, tp), cols].T)
            fthi[cols, pl.ds(i * tp, tp)] = hi
            ftlo[cols, pl.ds(i * tp, tp)] = lo

    def split_stored():
        s_load.wait()
        ts = min(32, n_st)

        @pl.loop(0, n_st // ts)
        def _(t):
            part = pl.ds(pl.multiple_of(t * ts, ts), ts)
            hi, lo = halves(s32v[part, :])
            shi[part, :] = hi
            slo[part, :] = lo

    def last_spread(r, ch):
        spread(r, ch, 1)
        rs_start(r, ch)

    def last_fitted(r, ch):
        fitted_partial(r, ch, 1)
        ar_core(r, ch)

    def first_spread(r, ch):
        ar_finish(r, ch)
        spread(r, ch, 0)

    def first_fitted(r, ch):
        ag_finish(r, ch)
        fitted_partial(r, ch, 0)

    def remainder(r, g):
        proj_done(r, g)
        removed(r, g)

    stages = {
        FACTOR: lambda _, i: split_factor(i),
        TURN: lambda _, i: turn_factor(i),
        STORED: lambda *_: split_stored(),
        SEND: ag_start,
        RELAY: ag_relay,
        FIT: first_fitted,
        FIT_B: last_fitted,
        SCATTER: ar_scatter,
        GATHER: ar_gather,
        SWAP: ar_swap,
        SPREAD: first_spread,
        SPREAD_B: last_spread,
        PASS: rs_relay,
        RESPOND: rs_finish,
        MEET: proj_start,
        MEET_Z: proj_middle,
        MEET_ALL: proj_finish,
        REMOVE: remainder,
        SQUARES: lambda r, _: squares_start(r),
        SQUARES_Z: lambda r, _: squares_middle(r),
        NORMS: lambda r, _: inverse_norms(r),
    }
    for stage, r, i in ORDER:
        stages[stage](r, i)
    o_next[...] = o_next[...] * invn[ROUNDS - 1, :, 0:1]

    for d in started:
        d.wait_send()
    for r in range(ROUNDS):
        for ch in range(CH):
            arrived(rbuf.at[r, ch, pl.ds(1, nxz - 1)], pr_s.at[r, ch])
            arrived(rbuf.at[r, ch, pl.ds(1, nxz - 1)], pa_s.at[r, ch])
        for g in range(GR):
            arrived(prx.at[r, g, pl.ds(1, nxc - 1)], px_s.at[r, g])
            arrived(prz.at[r, g, pl.ds(1, nz - 1)], pz_s.at[r, g])
            arrived(prx.at[r, g, pl.ds(1, nxc - 1)], py_s.at[r, g])
        arrived(srx.at[r, pl.ds(1, nxc - 1)], qx_s.at[r])
        arrived(srz.at[r, pl.ds(1, nz - 1)], qz_s.at[r])


def pr_cols(n_st):
    return -(-n_st // 256) * 128


def on_device(nx, nz, total_pairs, factor, trials, stored, gaps):
    pairs, aux = factor.shape
    rows = trials.shape[0]
    n_st = stored.shape[0]
    rc = rows // CH
    m, half = 4 * rc, 2 * rc
    rb, cb = half // nx, aux // nz
    nxc = 2 * nx
    gr = rows // GR
    pr, cw = gr // nx, pr_cols(n_st)
    V = pltpu.VMEM
    D = pltpu.SemaphoreType.DMA
    scratch = [
        V((pairs, aux), F32), V((pairs, aux), BF16), V((pairs, aux), BF16),
        V((aux, pairs), BF16), V((aux, pairs), BF16),
        V((n_st, pairs), F32), V((n_st, pairs), BF16), V((n_st, pairs), BF16),
        V((1, pairs), F32),
        V((ROUNDS, CH, 4, rc, pairs), F32),
        V((2 * m, pairs), BF16),
        V((ROUNDS, CH, m, aux), F32),
        V((ROUNDS, CH, half, aux), F32),
        V((ROUNDS, CH, half, aux), F32),
        V((ROUNDS, CH, nx * nz, rb, cb), F32),
        V((ROUNDS, CH, rb, cb), F32),
        V((ROUNDS, CH, m, aux), F32),
        V((2 * m, aux), BF16),
        V((ROUNDS, CH, 4, rc, pairs), F32),
        V((ROUNDS, CH, 2, rc // 2, pairs), F32),
        V((ROUNDS, CH, 2, rc, pairs), F32),
        V((rows, pairs), F32),
        V((2 * gr, pairs), BF16),
        V((ROUNDS, GR, gr, 2 * cw), F32),
        V((ROUNDS, GR, nxc, pr, cw), F32),
        V((ROUNDS, GR, pr, cw), F32),
        V((ROUNDS, GR, nz, pr, cw), F32),
        V((ROUNDS, GR, pr, cw), F32),
        V((ROUNDS, GR, gr, 2 * cw), F32),
        V((ROUNDS, nxc, 8, 128), F32),
        V((ROUNDS, 8, 128), F32),
        V((ROUNDS, nz, 8, 128), F32),
        V((ROUNDS, 8, 128), F32),
        V((ROUNDS, rows, 128), F32),
        V((ROUNDS, rows, 128), F32),
        D((CH + 6,)), D((ROUNDS, CH, 6)), D((ROUNDS, CH, 6)),
        D((ROUNDS, CH)), D((ROUNDS, CH)), D((ROUNDS, CH)), D((ROUNDS, CH)),
        D((ROUNDS, CH)), D((ROUNDS, CH)), D((ROUNDS, CH)), D((ROUNDS, CH)),
        D((ROUNDS, CH, 6)), D((ROUNDS, CH, 6)),
        D((ROUNDS, GR)), D((ROUNDS, GR)), D((ROUNDS, GR)), D((ROUNDS, GR)),
        D((ROUNDS, GR)), D((ROUNDS, GR)),
        D((ROUNDS,)), D((ROUNDS,)), D((ROUNDS,)), D((ROUNDS,)),
    ]
    any_spec = pl.BlockSpec(memory_space=pl.ANY)
    vmem_spec = pl.BlockSpec(memory_space=pltpu.VMEM)
    nxt, proj = pl.pallas_call(
        functools.partial(kernel, nx, nz, total_pairs),
        out_shape=(jax.ShapeDtypeStruct((rows, pairs), F32),
                   jax.ShapeDtypeStruct((ROUNDS, rows, n_st), F32)),
        in_specs=[any_spec] * 4,
        out_specs=(vmem_spec, vmem_spec),
        scratch_shapes=scratch,
        compiler_params=pltpu.CompilerParams(
            collective_id=0, has_side_effects=True, vmem_limit_bytes=66_000_000),
        name="response_rounds",
    )(factor, trials, stored, gaps.reshape(1, pairs))
    return nxt, jnp.swapaxes(proj, 1, 2)


def solution(mesh):
    nx, nz = 4, 8
    split = Mesh(
        mesh.devices.reshape(nx, nz, 2, mesh.shape["aux"]), ("x", "z", "core", "aux")
    )
    pair = ("x", "z", "core")
    return jax.shard_map(
        functools.partial(on_device, nx, nz, PAIRS),
        mesh=split,
        in_specs=(P(pair, "aux"), P("aux", pair), P(None, pair), P(pair)),
        out_specs=(P("aux", pair), P(None, None, "aux")),
        check_vma=False,
    )
```
